256 devices in a mesh: row: 16 (over x, y), col: 16 (over z, core).
Axes of the slice: x: 4, y: 4, z: 8, core: 2. Of those that a mesh axis runs over, the one named last changes fastest.
Arguments:
- coefficients: float32 [4096, 4096], P('row', 'col'), may hold values from -6 to 6
- diagonal: float32 [4096, 4096], P('row', 'col'), may hold values from 1.5 to 6
- energy_shift: float32 [1], replicated, may hold values from -1 to 0
- integrals: float32 [484, 484], replicated, may hold values from -0.25 to 0.25
- source_row: int32 [256, 128], P('row'), may hold values from 0 to 255
- target_row: int32 [256, 128], P('row'), may hold values from 0 to 7743
- phase_row: int32 [256, 128], P('row'), may hold values from -1 to 1, as said below
- source_col: int32 [256, 128], P('col'), may hold values from 0 to 255
- target_col: int32 [256, 128], P('col'), may hold values from 0 to 7743
- phase_col: int32 [256, 128], P('col'), may hold values from -1 to 1, as said below
Outputs:
- sigma_vector: float32 [4096, 4096], P('row', 'col')
- correction: float32 [4096, 4096], P('row', 'col')
The draws below stay inside these ranges and needn't reach their ends.
Inputs may be any that keep to these rules, and one draw needn't show every extreme that they name: `phase_row`: in each list row the entries with sign -1 or 1 come first and the rest are 0; in every draw some owner block receives all 128 slots live from every alpha block. `phase_col`: in each list row the entries with sign -1 or 1 come first and the rest are 0; in every draw some owner block receives all 128 slots live from every beta block.
All inputs are finite; a program needn't handle non-finite values.
Results may differ from the reference program's by a relative error of at most 0.000055.
Values sent between devices are 32-bit elements; how exact they have to be, the bound alone decides.
A program may use at most 64 MiB of HBM per device.

```python
import jax
import jax.numpy as jnp
from jax import lax

PAIRS = 484
ROWS_A = 256
COLS_B = 256
K_DEV = 16
CAP_A = 128
CAP_B = 128
NA = 4096
NB = 4096
N_ROW = 16
N_COL = 16


def live_phases(key, dev_count, capacity):
    key_full, key_level, key_sign = jax.random.split(key, 3)
    full_owner = jax.random.randint(key_full, (), 0, dev_count)
    levels = jax.random.randint(key_level, (dev_count, dev_count), 6, 17)
    owners = jnp.arange(dev_count)[None, :]
    levels = jnp.where(owners == full_owner, 16, levels)
    counts = capacity * levels // 16
    slot_ids = jnp.arange(capacity)[None, None, :]
    live = (slot_ids < counts[:, :, None]).astype(jnp.int32)
    signs = 2 * jax.random.randint(key_sign, (dev_count, dev_count, capacity), 0, 2) - 1
    return (live * signs).reshape(dev_count * dev_count, capacity).astype(jnp.int32)


def draw_phase_row(key, part):
    return live_phases(jax.random.fold_in(key, 11), N_ROW, CAP_A)


def draw_phase_col(key, part):
    return live_phases(jax.random.fold_in(key, 23), N_COL, CAP_B)


def with_ends(entries, key, low, top_value):
    shape = entries.shape
    index_at = [jax.random.randint(jax.random.fold_in(key, axis), (), 0, shape[axis]) for axis in range(len(shape))]
    entries = entries.at[tuple(index_at)].set(low)
    longest = shape.index(max(shape))
    index_at[longest] = (index_at[longest] + 1) % shape[longest]
    return entries.at[tuple(index_at)].set(top_value)


def block_levels(stream_key, dims, cuts, smallest, largest):
    gain = 1.0
    for dim, blocks in cuts:
        steps = jax.random.uniform(jax.random.fold_in(jax.random.fold_in(stream_key, 6), dim), (blocks,), jnp.float32, smallest / len(cuts), largest / len(cuts))
        gain = gain * jnp.repeat(jnp.exp(steps), dims[dim] // blocks).reshape((-1,) + (1,) * (len(dims) - 1 - dim))
    return gain


def noise(rng, dims, scale, reach, pieces=(), kind=jnp.bfloat16):
    entries = jax.random.normal(rng, dims, jnp.float32) * scale
    if len(pieces) > 0:
        entries = block_levels(rng, dims, pieces, -0.22, 0.18) * entries
    return jnp.clip(entries, min=-reach, max=reach).astype(kind)


def setup_inputs(seed: int = 0) -> dict:
    seeds = jax.random.split(jax.random.key(seed), 11)
    return {
        "coefficients": noise(seeds[0], (NA, NB), 1.0, 6.0, ((0, 16), (1, 16)), jnp.float32),
        "diagonal": jnp.clip(1.5 + 4.5 * jax.random.uniform(seeds[1], (NA, NB), jnp.float32) ** block_levels(seeds[1], (NA, NB), ((0, 16), (1, 16)), -0.2, 0.2), 1.5, 6.0),
        "energy_shift": jnp.clip(jax.random.uniform(seeds[2], (1,), jnp.float32, -1.0, 0.0), -1.0, 0.0),
        "integrals": noise(seeds[3], (PAIRS, PAIRS), PAIRS ** -0.5, 0.25, (), jnp.float32),
        "source_row": with_ends(jax.random.randint(seeds[4], (N_ROW * N_ROW, CAP_A), 0, ROWS_A), jax.random.fold_in(seeds[4], 1), 0, ROWS_A - 1).astype(jnp.int32),
        "target_row": with_ends(jax.random.randint(seeds[5], (N_ROW * N_ROW, CAP_A), 0, K_DEV * PAIRS), jax.random.fold_in(seeds[5], 1), 0, (K_DEV * PAIRS) - 1).astype(jnp.int32),
        "phase_row": draw_phase_row(jax.random.fold_in(seeds[10], 71), 0),
        "source_col": with_ends(jax.random.randint(seeds[7], (N_COL * N_COL, CAP_B), 0, COLS_B), jax.random.fold_in(seeds[7], 1), 0, COLS_B - 1).astype(jnp.int32),
        "target_col": with_ends(jax.random.randint(seeds[8], (N_COL * N_COL, CAP_B), 0, K_DEV * PAIRS), jax.random.fold_in(seeds[8], 1), 0, (K_DEV * PAIRS) - 1).astype(jnp.int32),
        "phase_col": draw_phase_col(jax.random.fold_in(seeds[10], 71), 0),
    }


def same_spin(matrix, source, target, phases, dev_count, rows_dev, block_cols, block_count, integrals):
    total_rows = matrix.shape[0]
    pair_count = integrals.shape[0]
    list_index = jnp.arange(dev_count * dev_count).astype(jnp.int32)
    owner = list_index % dev_count
    sender = list_index // dev_count
    global_row = (sender[:, None] * rows_dev + source).reshape(-1).astype(jnp.int32)
    slot_index = (owner[:, None] * (K_DEV * pair_count) + target).reshape(-1).astype(jnp.int32)
    signs = phases.reshape(-1).astype(jnp.float32)

    def one_block(index):
        columns = lax.dynamic_slice_in_dim(matrix, index * block_cols, block_cols, 1)
        signed = columns[global_row] * signs[:, None]
        densities = jnp.zeros((dev_count * K_DEV * pair_count, block_cols), jnp.float32).at[slot_index].add(signed)
        products = jnp.einsum("ip,kpb->kib", integrals, densities.reshape(-1, pair_count, block_cols),
                              precision=lax.Precision.HIGHEST).reshape(-1, block_cols)
        picked = products[slot_index] * signs[:, None]
        return jnp.zeros((total_rows, block_cols), jnp.float32).at[global_row].add(picked)

    blocks = lax.map(one_block, jnp.arange(block_count).astype(jnp.int32))
    return jnp.transpose(blocks, (1, 0, 2)).reshape(total_rows, block_count * block_cols)


def reference(coefficients, diagonal, energy_shift, integrals, source_row, target_row, phase_row, source_col, target_col, phase_col):
    alpha_part = same_spin(coefficients, source_row, target_row, phase_row, N_ROW, ROWS_A, COLS_B, N_COL, integrals)
    beta_part = same_spin(coefficients.T, source_col, target_col, phase_col, N_COL, COLS_B, ROWS_A, N_ROW, integrals)
    sigma_vector = alpha_part + beta_part.T
    correction = (sigma_vector - energy_shift[0] * coefficients) / (diagonal - energy_shift[0])
    return sigma_vector, correction
```

```python
import functools

import jax
import jax.numpy as jnp
from jax import lax
from jax.experimental import pallas as pl
from jax.experimental.pallas import tpu as pltpu
from jax.sharding import PartitionSpec as P

MESH = pl.DeviceIdType.MESH
NX, NY, NZ = 4, 4, 8
PAIRS = 484
PPAD = 512
BLK = 256
CAP = 128
LISTS = 16
F32, BF16, I32 = jnp.float32, jnp.bfloat16, jnp.int32


class Copy:
    def __init__(self, buf, q, rel, rows, way, deps):
        self.buf, self.q, self.rel, self.rows, self.way, self.deps = buf, q, rel, rows, way, deps
        self.number = None

    def arriving(self):
        first, second = self.rel
        if self.way == "s":
            return (first, 1 - second)
        axis, step = self.way[0], 1 if self.way[1] == "+" else -1
        if axis in "xz":
            return (first - step, second)
        return (first, second - step)


def plane_copies(q):
    copies = []

    def add(*args):
        copies.append(Copy("x", q, *args))
        return copies[-1]

    for half, (f, g) in enumerate((("x", "y"), ("y", "x"))):
        base = half * 128
        rows, low, high = (base, 128), (base, 64), (base + 64, 64)

        def at(df, dg, f=f):
            return (df, dg) if f == "x" else (dg, df)

        own_f = [add(at(0, 0), rows, f + s, [("own", q)]) for s in "+-"]
        minus, plus = own_f
        spread = [(0, [("own", q)])]
        fwd = [add(at(-1, 0), low, f + "+", [minus]), add(at(1, 0), high, f + "-", [plus])]
        spread += [(-1, [minus]), (1, [plus]), (2, fwd)]
        for d, deps in spread:
            up = add(at(d, 0), rows, g + "+", deps)
            down = add(at(d, 0), rows, g + "-", deps)
            add(at(d, -1), low, g + "+", [up])
            add(at(d, 1), high, g + "-", [down])
    return copies


def ring_copies(q):
    copies = []

    def add(*args):
        copies.append(Copy("z", q, *args))
        return copies[-1]

    whole = (0, 256)
    have = {0: [("own", q)]}
    add((0, 0), whole, "s", [("own", q)])
    last = {}
    for half in range(2):
        rows = (half * 128, 128)
        for s, sign in (("+", -1), ("-", 1)):
            dep = [("own", q)]
            for t in range(3):
                copy = add((sign * t, 0), rows, "z" + s, dep)
                dep = [copy]
                have.setdefault(sign * (t + 1), []).append(copy)
            last[(half, s)] = dep
    far = [add((-3, 0), (0, 128), "z+", last[(0, "+")]), add((3, 0), (128, 128), "z-", last[(1, "-")])]
    have[4] = far
    for d in (-1, 1, -2, 2, -3, 3, 4):
        add((d, 0), whole, "s", have[d])
    return copies


RATE = {"x": 46.0, "y": 46.0, "z": 46.0, "s": 150.0}
HOP = 1.8


def simulate(copies, own_time):
    ready_at = {}
    free = {}
    arrivals = {}
    pending = list(copies)
    order = []
    while pending:
        best = None
        for copy in pending:
            t = 0.0
            for dep in copy.deps:
                when = own_time[dep[1]] if isinstance(dep, tuple) else arrivals.get(dep.number)
                if when is None:
                    t = None
                    break
                t = max(t, when)
            if t is None:
                continue
            if best is None or (t, copy.number) < best[:2]:
                best = (t, copy.number, copy)
        t, _, copy = best
        start = max(t, free.get(copy.way, 0.0))
        lasting = copy.rows[1] * BLK * 4 / RATE[copy.way[0]] / 1e3
        free[copy.way] = start + lasting
        arrivals[copy.number] = start + lasting + HOP
        order.append(copy.number)
        pending.remove(copy)
    return arrivals, order


J_US, T_US, LEAD_US = 0.7, 0.45, 3.0
N_J, N_T = 16, 32


def make_plan():
    copies = plane_copies(0) + ring_copies(0) + plane_copies(1) + ring_copies(1)
    for n, copy in enumerate(copies):
        copy.number = n
    done_t = LEAD_US + N_J * J_US + N_T * T_US
    arrivals, _ = simulate(copies, {0: 0.0, 1: done_t})
    events = sorted(copies, key=lambda c: (arrivals[c.number], c.number))
    complete = {}
    for copy in copies:
        key = (copy.buf, copy.q, norm(copy.buf, copy.arriving()))
        complete[key] = max(complete.get(key, 0.0), arrivals[copy.number])
    steps = []
    for buf, mod in (("x", None), ("z", None)):
        rels = plane_rels() if buf == "x" else ring_rels()
        for rel in rels:
            ready = complete.get((buf, 1, rel), done_t)
            steps.append((ready, buf, rel))
    steps.sort(key=lambda s: (s[0], s[1], s[2]))
    return copies, arrivals, events, steps, done_t


def norm(buf, rel):
    if buf == "x":
        return (rel[0] % NX, rel[1] % NY)
    return (rel[0] % NZ, rel[1])


def plane_rels():
    return [(i, j) for i in range(NX) for j in range(NY)]


def ring_rels():
    return [(i, j) for i in range(NZ) for j in range(2)]


def split(v):
    high = v.astype(BF16)
    return high, (v - high.astype(F32)).astype(BF16)


def one_hot_rows(index_row, rows, weight=None):
    hit = lax.broadcasted_iota(I32, (rows, index_row.shape[1]), 0) == index_row
    value = 1.0 if weight is None else weight
    return jnp.where(hit, value, 0.0).astype(BF16)


def slot_of(target):
    return (target * 4333) >> 21


def kernel(
    plan,
    shift_ref, c_ref, diag_ref, int_ref,
    src_r, tgt_r, ph_r, src_c, tgt_c, ph_c,
    sigma_ref, corr_ref,
    gx, gz, ipad, ihl, own, oth, jmat, amat, tcol, tacc, acc,
    send_sem, recv_sem, list_send, list_recv,
):
    copies, arrivals, events, steps, done_t = plan
    r, c = lax.axis_index("row"), lax.axis_index("col")
    x, y = r // NY, lax.rem(r, NY)
    z, k = c // 2, lax.rem(c, 2)

    def row_at(dx, dy):
        return lax.rem(x + (dx + NX) % NX, NX) * NY + lax.rem(y + (dy + NY) % NY, NY)

    def col_at(dz, flip):
        return lax.rem(z + (dz + NZ) % NZ, NZ) * 2 + (lax.rem(k + 1, 2) if flip else k)

    def place(buf, rel):
        return row_at(*rel) if buf == "x" else col_at(*rel)

    def device(way):
        if way == "s":
            return (r, col_at(0, 1))
        d = 1 if way[1] == "+" else -1
        if way[0] == "x":
            return (row_at(d, 0), c)
        if way[0] == "y":
            return (row_at(0, d), c)
        return (r, col_at(d, 0))

    bufs = {"x": gx, "z": gz}

    def describe(copy, rel):
        where = bufs[copy.buf].at[copy.q, place(copy.buf, rel), pl.ds(*copy.rows)]
        return pltpu.make_async_remote_copy(
            src_ref=where, dst_ref=where,
            send_sem=send_sem.at[copy.number], recv_sem=recv_sem.at[copy.number],
            device_id=device(copy.way), device_id_type=MESH,
        )

    arrived = set()
    started = set()

    def start_ready():
        for copy in copies:
            if copy.number in started:
                continue
            if all((dep if isinstance(dep, tuple) else dep.number) in arrived for dep in copy.deps):
                started.add(copy.number)
                describe(copy, copy.rel).start()

    def take(copy):
        describe(copy, copy.arriving()).wait_recv()
        arrived.add(copy.number)
        start_ready()

    queue = list(events)

    def pop_until(t):
        out = []
        while queue and arrivals[queue[0].number] <= t:
            out.append(queue.pop(0))
        return out

    barrier = pltpu.get_barrier_semaphore()
    others = ["x+", "x-", "y+", "y-", "z+", "z-", "s"]
    partner = (c, r)
    for way in others:
        pl.semaphore_signal(barrier, inc=1, device_id=device(way), device_id_type=MESH)

    @pl.when(r != c)
    def _():
        pl.semaphore_signal(barrier, inc=1, device_id=partner, device_id_type=MESH)

    gx[0, r] = c_ref[...]
    gz[0, c] = c_ref[...]

    @pl.when(r != c)
    def _():
        pl.semaphore_wait(barrier, len(others) + 1)

    @pl.when(r == c)
    def _():
        pl.semaphore_wait(barrier, len(others))

    lists = (src_r, tgt_r, ph_r, src_c, tgt_c, ph_c)

    def list_copy(n):
        return pltpu.make_async_remote_copy(
            src_ref=lists[n], dst_ref=oth.at[n // 3, n % 3],
            send_sem=list_send.at[n], recv_sem=list_recv.at[n],
            device_id=partner, device_id_type=MESH,
        )

    @pl.when(r != c)
    def _():
        for n in range(6):
            list_copy(n).start()

    arrived.add(("own", 0))
    start_ready()

    for n in range(6):
        own[n // 3, n % 3] = lists[n][...]
    ipad[...] = jnp.zeros_like(ipad)
    ipad[0:PAIRS, 0:PAIRS] = int_ref[...]
    high, low = split(ipad[...].T)
    ihl[0:PPAD, :] = high
    ihl[PPAD:, :] = low
    tacc[...] = jnp.zeros_like(tacc)

    slots_j = {}
    for n in range(N_J):
        slots_j[n] = pop_until(LEAD_US + (n + 1) * J_US)

    def j_step(it, carry):
        side, o0 = it // 8, 2 * lax.rem(it, 8)
        rows = []
        for d in range(2):
            t = own[side, 1, pl.ds(o0 + d, 1), :]
            rows.append(t - PAIRS * slot_of(t))
            hot = one_hot_rows(own[side, 0, pl.ds(o0 + d, 1), :], BLK, own[side, 2, pl.ds(o0 + d, 1), :].astype(F32))
            amat[side, o0 + d, :, 0:CAP] = hot
            amat[side, o0 + d, :, CAP:] = hot
        hot = one_hot_rows(jnp.concatenate(rows, axis=1), PPAD)
        for part in range(2):
            prod = jnp.dot(ihl[pl.ds(part * PPAD, PPAD), :], hot, preferred_element_type=F32).astype(BF16)
            for d in range(2):
                jmat[side, o0 + d, :, part * CAP:(part + 1) * CAP] = prod[:, d * CAP:(d + 1) * CAP]
        for n, evs in slots_j.items():
            if evs:
                @pl.when(it == n)
                def _(evs=evs):
                    for copy in evs:
                        take(copy)
        return carry

    lax.fori_loop(0, N_J, j_step, 0)

    @pl.when(r != c)
    def _():
        for n in range(6):
            list_copy(n).wait()

    @pl.when(r == c)
    def _():
        for n in range(6):
            oth[n // 3, n % 3] = lists[n][...]

    for side in range(2):
        t = jnp.concatenate([oth[side, 1].astype(F32), jnp.zeros((CAP - LISTS, CAP), F32)], axis=0).T.astype(I32)
        for o in range(LISTS):
            tcol[side, o] = jnp.broadcast_to(t[:, o:o + 1], (CAP, CAP))

    slots_t = {}
    for n in range(N_T):
        slots_t[n] = pop_until(LEAD_US + N_J * J_US + (n + 1) * T_US)

    def t_step(it, carry):
        side, o = it // 16, lax.rem(it, 16)
        t = tcol[side, o]
        kc = slot_of(t)
        pc = t - PAIRS * kc
        lane = lax.broadcasted_iota(I32, (CAP, CAP), 1)
        hot = jnp.concatenate(
            [jnp.where(pc - CAP * m == lane, 1.0, 0.0).astype(BF16) for m in range(PPAD // CAP)], axis=1
        )
        g = jnp.dot(hot, jmat[side, o], preferred_element_type=F32)
        same = kc == slot_of(own[side, 1, pl.ds(o, 1), :])
        w = jnp.concatenate(
            [jnp.where(same, g[:, 0:CAP], 0.0).astype(BF16), jnp.where(same, g[:, CAP:], 0.0).astype(BF16)], axis=1
        )
        u = lax.dot_general(w, amat[side, o], (((1,), (1,)), ((), ())), preferred_element_type=F32)
        uh, ul = split(u)
        hot = one_hot_rows(oth[side, 0, pl.ds(o, 1), :], BLK, oth[side, 2, pl.ds(o, 1), :].astype(F32))
        tacc[side] += jnp.dot(
            jnp.concatenate([hot, hot], axis=1), jnp.concatenate([uh, ul], axis=0), preferred_element_type=F32
        )
        for n, evs in slots_t.items():
            if evs:
                @pl.when(it == n)
                def _(evs=evs):
                    for copy in evs:
                        take(copy)
        return carry

    lax.fori_loop(0, N_T, t_step, 0)

    gz[1, c] = tacc[0].T
    gx[1, r] = tacc[1]
    arrived.add(("own", 1))
    start_ready()
    for copy in [e for e in queue if e.q == 0]:
        take(copy)
    queue[:] = [e for e in queue if e.q == 1]

    acc[...] = jnp.zeros_like(acc)
    slots_f = {}
    for n, (ready, buf, rel) in enumerate(steps):
        slots_f[n] = pop_until(ready if n < len(steps) - 1 else 1e9)

    def f_step(it, carry):
        for n, evs in slots_f.items():
            if evs:
                @pl.when(it == n)
                def _(evs=evs):
                    for copy in evs:
                        take(copy)
        index = 0
        which = 0
        for n, (_, buf, rel) in enumerate(steps):
            index = jnp.where(it == n, place(buf, rel), index)
            which = jnp.where(it == n, 1 if buf == "x" else 0, which)
        left_high, left_low = split(gz[1 - which, index])
        right_high, right_low = split(gx[which, index])
        acc[...] += jnp.dot(
            jnp.concatenate([left_high, left_high, left_low], axis=1),
            jnp.concatenate([right_high, right_low, right_high], axis=0),
            preferred_element_type=F32,
        )
        return carry

    lax.fori_loop(0, len(steps), f_step, 0)

    sigma = acc[...]
    sigma_ref[...] = sigma
    shift = shift_ref[0]
    corr_ref[...] = (sigma - shift * c_ref[...]) / (diag_ref[...] - shift)

    for copy in copies:
        describe(copy, copy.rel).wait_send()


def shards(coefficients, diagonal, energy_shift, integrals, source_row, target_row, phase_row,
           source_col, target_col, phase_col):
    plan = make_plan()
    n_copies = len(plan[0])
    vmem = pl.BlockSpec(memory_space=pltpu.VMEM)
    out = jax.ShapeDtypeStruct((BLK, BLK), F32)
    return pl.pallas_call(
        functools.partial(kernel, plan),
        out_shape=(out, out),
        in_specs=[pl.BlockSpec(memory_space=pltpu.SMEM)] + [vmem] * 9,
        out_specs=(vmem, vmem),
        scratch_shapes=[
            pltpu.VMEM((2, 16, BLK, BLK), F32),
            pltpu.VMEM((2, 16, BLK, BLK), F32),
            pltpu.VMEM((PPAD, PPAD), F32),
            pltpu.VMEM((2 * PPAD, PPAD), BF16),
            pltpu.VMEM((2, 3, LISTS, CAP), I32),
            pltpu.VMEM((2, 3, LISTS, CAP), I32),
            pltpu.VMEM((2, LISTS, PPAD, 2 * CAP), BF16),
            pltpu.VMEM((2, LISTS, BLK, 2 * CAP), BF16),
            pltpu.VMEM((2, LISTS, CAP, CAP), I32),
            pltpu.VMEM((2, BLK, BLK), F32),
            pltpu.VMEM((BLK, BLK), F32),
            pltpu.SemaphoreType.DMA((n_copies,)),
            pltpu.SemaphoreType.DMA((n_copies,)),
            pltpu.SemaphoreType.DMA((6,)),
            pltpu.SemaphoreType.DMA((6,)),
        ],
        compiler_params=pltpu.CompilerParams(
            collective_id=0, has_side_effects=True, vmem_limit_bytes=60 * 1024 * 1024
        ),
    )(energy_shift, coefficients, diagonal, integrals, source_row, target_row, phase_row,
      source_col, target_col, phase_col)


def solution(mesh):
    in_specs = (
        P("row", "col"),
        P("row", "col"),
        P(),
        P(),
        P("row", None),
        P("row", None),
        P("row", None),
        P("col", None),
        P("col", None),
        P("col", None),
    )
    out_specs = (P("row", "col"), P("row", "col"))
    return jax.shard_map(shards, mesh=mesh, in_specs=in_specs, out_specs=out_specs, check_vma=False)
```

```python
import functools

import jax
import jax.numpy as jnp
from jax import lax
from jax.experimental import pallas as pl
from jax.experimental.pallas import tpu as pltpu
from jax.sharding import PartitionSpec as P

MESH = pl.DeviceIdType.MESH
NX, NY, NZ = 4, 4, 8
PAIRS = 484
PPAD = 512
BLK = 256
CAP = 128
LISTS = 16
F32, BF16, I32 = jnp.float32, jnp.bfloat16, jnp.int32


class Copy:
    def __init__(self, buf, q, rel, rows, way, deps):
        self.buf, self.q, self.rel, self.rows, self.way, self.deps = buf, q, rel, rows, way, deps
        self.number = None

    def arriving(self):
        rel = list(self.rel)
        if self.way == "s":
            rel[1] = 1 - rel[1]
        elif self.q == 1:
            rel[0] = 1 - rel[0]
        else:
            step = 1 if self.way[1] == "+" else -1
            rel[0 if self.way[0] in "xz" else 1] -= step
        return tuple(rel)


WHOLE = (0, BLK)


def plane_copies():
    copies = []

    def add(*args):
        copies.append(Copy("x", 0, *args))
        return copies[-1]

    for half, (f, g) in enumerate((("x", "y"), ("y", "x"))):
        base = half * 128
        rows, low, high = (base, 128), (base, 64), (base + 64, 64)

        def at(df, dg, f=f):
            return (df, dg) if f == "x" else (dg, df)

        own_f = [add(at(0, 0), rows, f + s, ["C"]) for s in "+-"]
        minus, plus = own_f
        spread = [(0, ["C"])]
        fwd = [add(at(-1, 0), low, f + "+", [minus]), add(at(1, 0), high, f + "-", [plus])]
        spread += [(-1, [minus]), (1, [plus]), (2, fwd)]
        for d, deps in spread:
            up = add(at(d, 0), rows, g + "+", deps)
            down = add(at(d, 0), rows, g + "-", deps)
            add(at(d, -1), low, g + "+", [up])
            add(at(d, 1), high, g + "-", [down])
    return copies


def ring_copies():
    copies = []

    def add(*args):
        copies.append(Copy("z", 0, *args))
        return copies[-1]

    have = {}
    add((0, 0), WHOLE, "s", ["C"])
    last = {}
    for half in range(2):
        rows = (half * 128, 128)
        for s, sign in (("+", -1), ("-", 1)):
            dep = ["C"]
            for t in range(3):
                copy = add((sign * t, 0), rows, "z" + s, dep)
                dep = [copy]
                have.setdefault(sign * (t + 1), []).append(copy)
            last[(half, s)] = dep
    have[4] = [add((-3, 0), (0, 128), "z+", last[(0, "+")]), add((3, 0), (128, 128), "z-", last[(1, "-")])]
    for d in (-1, 1, -2, 2, -3, 3, 4):
        add((d, 0), WHOLE, "s", have[d])
    return copies, {"z+": last[(0, "+")] + last[(1, "+")], "z-": last[(0, "-")] + last[(1, "-")]}


def block_copies(last):
    copies = []
    for j in range(GROUP):
        way = "z+" if j % 2 == 0 else "z-"
        far = Copy("z", 1, (0, 0, j), WHOLE, way, ["T0"] + last[way])
        copies += [far, Copy("z", 1, (0, 0, j), WHOLE, "s", ["T0"]), Copy("z", 1, (1, 0, j), WHOLE, "s", [far])]
    for j in range(2 * GROUP):
        way = ("x+", "x-", "y+", "y-")[j % 4]
        copies.append(Copy("x", 1, (0, j), WHOLE, way, ["T%d" % (1 + j // GROUP)]))
    return copies


RATE = {"x": 46.8, "y": 46.8, "z": 46.8, "s": 350.0}
HOP = 1.8


def simulate(copies, own_time):
    free, arrivals, pending = {}, {}, list(copies)
    while pending:
        best = None
        for copy in pending:
            times = [own_time[dep] if isinstance(dep, str) else arrivals.get(dep.number) for dep in copy.deps]
            if None in times:
                continue
            if best is None or (max(times), copy.number) < best[:2]:
                best = (max(times), copy.number, copy)
        t, _, copy = best
        start = max(t, free.get(copy.way, 0.0))
        lasting = copy.rows[1] * BLK * 4 / RATE[copy.way[0]] / 1e3
        free[copy.way] = start + lasting
        arrivals[copy.number] = start + lasting + HOP
        pending.remove(copy)
    return arrivals


GROUP = 4
PHASES = 3
N_J, J_US = 8, 0.8
N_T, T_US = 16 * PHASES, 0.5
LIST_US = 5.0
T0_US = N_J * J_US + 2.5


def make_plan():
    ring, last = ring_copies()
    copies = plane_copies() + ring + block_copies(last)
    for n, copy in enumerate(copies):
        copy.number = n
    own_time = {"C": 0.0}
    for p in range(PHASES):
        own_time["T%d" % p] = T0_US + (p + 1) * 16 * T_US
    arrivals = simulate(copies, own_time)
    events = sorted(copies, key=lambda c: (arrivals[c.number], c.number))
    ready = {}
    for copy in copies:
        if copy.q == 1:
            ready[(copy.buf, copy.arriving())] = arrivals[copy.number]
    steps = []
    for j in range(GROUP):
        steps.append((own_time["T0"], "z", (0, 0, j)))
    for j in range(2 * GROUP):
        steps.append((own_time["T%d" % (1 + j // GROUP)], "x", (0, j)))
    steps += [(when, buf, rel) for (buf, rel), when in ready.items()]
    steps.sort(key=lambda s: (s[0], s[1], s[2]))
    return copies, arrivals, events, steps


def split(v):
    high = v.astype(BF16)
    return high, (v - high.astype(F32)).astype(BF16)


def one_hot_rows(index_row, rows, weight=None):
    hit = lax.broadcasted_iota(I32, (rows, index_row.shape[1]), 0) == index_row
    value = 1.0 if weight is None else weight
    return jnp.where(hit, value, 0.0).astype(BF16)


def slot_of(target):
    return (target * 4333) >> 21


def kernel(
    plan,
    shift_ref, c_ref, diag_ref, int_ref,
    src_r, tgt_r, ph_r, src_c, tgt_c, ph_c,
    sigma_ref, corr_ref,
    gx, gz, ints, diag, ipad, ihl, own, oth, jmat, amat, tcol, tacc, acc,
    load_sem, send_sem, recv_sem, a_send, a_recv, b_send, b_recv, f_send,
):
    copies, arrivals, events, steps = plan
    r, c = lax.axis_index("row"), lax.axis_index("col")
    x, y = r // NY, lax.rem(r, NY)
    z, k = c // 2, lax.rem(c, 2)
    zpar, xpar = lax.rem(z, 2), lax.rem(x + y, 2)

    def flip(v, by):
        return 1 - v if by else v

    def row_at(dx, dy):
        return lax.rem(x + (dx + NX) % NX, NX) * NY + lax.rem(y + (dy + NY) % NY, NY)

    def col_at(dz, by):
        return lax.rem(z + (dz + NZ) % NZ, NZ) * 2 + flip(k, by)

    def place(buf, q, rel):
        if q == 0:
            return row_at(*rel) if buf == "x" else col_at(*rel)
        if buf == "x":
            return 2 * GROUP * flip(xpar, rel[0]) + rel[1]
        return 2 * GROUP * flip(zpar, rel[0]) + GROUP * flip(k, rel[1]) + rel[2]

    def device(way):
        if way == "s":
            return (r, col_at(0, 1))
        d = 1 if way[1] == "+" else -1
        if way[0] == "x":
            return (row_at(d, 0), c)
        if way[0] == "y":
            return (row_at(0, d), c)
        return (r, col_at(d, 0))

    bufs = {"x": gx, "z": gz}

    def describe(copy, rel):
        where = bufs[copy.buf].at[copy.q, place(copy.buf, copy.q, rel), pl.ds(*copy.rows)]
        return pltpu.make_async_remote_copy(
            src_ref=where, dst_ref=where,
            send_sem=send_sem.at[copy.number], recv_sem=recv_sem.at[copy.number],
            device_id=device(copy.way), device_id_type=MESH,
        )

    arrived, started = set(), set()

    def start_ready():
        for copy in copies:
            if copy.number in started:
                continue
            if all((dep if isinstance(dep, str) else dep.number) in arrived for dep in copy.deps):
                started.add(copy.number)
                describe(copy, copy.rel).start()

    def have(name):
        arrived.add(name)
        start_ready()

    def take(copy):
        describe(copy, copy.arriving()).wait_recv()
        have(copy.number)

    queue = list(events)

    def pop_until(t):
        out = []
        while queue and arrivals[queue[0].number] <= t:
            out.append(queue.pop(0))
        return out

    def at_step(it, slots):
        for n, evs in slots.items():
            if evs:
                @pl.when(it == n)
                def _(evs=evs):
                    for copy in evs:
                        if callable(copy):
                            copy()
                        else:
                            take(copy)

    lists = (src_r, tgt_r, ph_r, src_c, tgt_c, ph_c)
    loads = [pltpu.make_async_copy(lists[n], own.at[n // 3, n % 3], load_sem.at[n]) for n in range(6)]
    loads.append(pltpu.make_async_copy(c_ref, gx.at[0, r], load_sem.at[6]))
    loads.append(pltpu.make_async_copy(c_ref, gz.at[0, c], load_sem.at[7]))
    loads.append(pltpu.make_async_copy(int_ref, ints, load_sem.at[8]))
    loads.append(pltpu.make_async_copy(diag_ref, diag, load_sem.at[9]))
    for load in loads:
        load.start()

    plane = [(dx, dy) for dx in range(NX) for dy in range(NY) if (dx, dy) != (0, 0)]
    peers = [(row_at(*rel), c) for rel in plane] + [(r, col_at(d, 0)) for d in range(1, NZ)] + [(r, col_at(0, 1))]
    barrier = pltpu.get_barrier_semaphore()
    for peer in peers:
        pl.semaphore_signal(barrier, inc=1, device_id=peer, device_id_type=MESH)
    for load in loads[:8]:
        load.wait()
    pl.semaphore_wait(barrier, len(peers))

    ax = 2 * zpar + k
    bz = (NZ // 2) * xpar
    in_a = x == ax
    in_b = z // (NZ // 2) == xpar

    def a_copy(n, slot):
        return pltpu.make_async_remote_copy(
            src_ref=own.at[0], dst_ref=oth.at[slot], send_sem=a_send.at[n], recv_sem=a_recv.at[slot],
            device_id=(row_at(*plane[n]), c), device_id_type=MESH,
        )

    def b_copy(n, jz):
        return pltpu.make_async_remote_copy(
            src_ref=own.at[1], dst_ref=oth.at[GROUP + 2 * jz + k], send_sem=b_send.at[n],
            recv_sem=b_recv.at[2 * jz + k],
            device_id=(r, col_at(n + 1, 0)), device_id_type=MESH,
        )

    def f_copy(jz, core, mine):
        slot = 2 * jz + core
        return pltpu.make_async_remote_copy(
            src_ref=own.at[1] if mine else oth.at[GROUP + slot], dst_ref=oth.at[GROUP + slot],
            send_sem=f_send.at[jz], recv_sem=b_recv.at[slot],
            device_id=(r, col_at(0, 1)), device_id_type=MESH,
        )

    @pl.when(in_b)
    def _():
        for n in range(NZ - 1):
            b_copy(n, z - bz).start()

    @pl.when(in_a)
    def _():
        for n in range(len(plane)):
            a_copy(n, y).start()

    have("C")

    def forward_lists():
        for jz in range(NZ // 2):
            @pl.when(z == bz + jz)
            def _(jz=jz):
                f_copy(jz, k, True).start()

            @pl.when(z != bz + jz)
            def _(jz=jz):
                b_copy(0, jz).wait_recv()
                f_copy(jz, k, False).start()

    ipad[...] = jnp.zeros_like(ipad)
    loads[8].wait()
    ipad[0:PAIRS, 0:PAIRS] = ints[...]
    high, low = split(ipad[...].T)
    ihl[0:PPAD, :] = high
    ihl[PPAD:, :] = low
    tacc[...] = jnp.zeros_like(tacc)

    slots_j = {n: pop_until((n + 1) * J_US) for n in range(N_J)}
    slots_j[min(N_J - 1, int(LIST_US / J_US))].append(forward_lists)

    def j_step(it, carry):
        side, o0 = it // (N_J // 2), 4 * lax.rem(it, N_J // 2)
        rows = []
        for d in range(4):
            t = own[side, 1, pl.ds(o0 + d, 1), :]
            rows.append(t - PAIRS * slot_of(t))
            hot = one_hot_rows(own[side, 0, pl.ds(o0 + d, 1), :], BLK, own[side, 2, pl.ds(o0 + d, 1), :].astype(F32))
            amat[side, o0 + d, :, 0:CAP] = hot
            amat[side, o0 + d, :, CAP:] = hot
        hot = one_hot_rows(jnp.concatenate(rows, axis=1), PPAD)
        for part in range(2):
            prod = jnp.dot(ihl[pl.ds(part * PPAD, PPAD), :], hot, preferred_element_type=F32).astype(BF16)
            for d in range(4):
                jmat[side, o0 + d, :, part * CAP:(part + 1) * CAP] = prod[:, d * CAP:(d + 1) * CAP]
        at_step(it, slots_j)
        return carry

    lax.fori_loop(0, N_J, j_step, 0)

    for j in range(GROUP):
        @pl.when(jnp.logical_not(in_a & (y == j)))
        def _(j=j):
            a_copy(0, j).wait_recv()
    for jz in range(NZ // 2):
        f_copy(jz, 1 - k, False).wait_recv()

    @pl.when(in_a)
    def _():
        oth[y] = own[0]

    @pl.when(in_b)
    def _():
        oth[GROUP + 2 * (z - bz) + k] = own[1]

    def turn(b, carry):
        t = jnp.concatenate([oth[b, 1].astype(F32), jnp.zeros((CAP - LISTS, CAP), F32)], axis=0).T.astype(I32)
        for o in range(LISTS):
            tcol[b, o] = jnp.broadcast_to(t[:, o:o + 1], (CAP, CAP))
        return carry

    lax.fori_loop(0, GROUP * PHASES, turn, 0)

    slots_t = {n: pop_until(T0_US + (n + 1) * T_US) for n in range(N_T)}

    def finish(p):
        def act():
            for j in range(GROUP):
                if p == 0:
                    gz[1, place("z", 1, (0, 0, j))] = tacc[j].T
                else:
                    gx[1, place("x", 1, (0, GROUP * (p - 1) + j))] = tacc[GROUP * p + j]
            have("T%d" % p)
        return act

    for p in range(PHASES):
        slots_t[16 * p + 15].insert(0, finish(p))

    def t_step(it, carry):
        p, o = it // 16, lax.rem(it, 16)
        side = jnp.minimum(p, 1)
        lane = lax.broadcasted_iota(I32, (CAP, CAP), 1)
        slots, hots = [], []
        for j in range(GROUP):
            t = tcol[GROUP * p + j, o]
            kc = slot_of(t)
            pc = t - PAIRS * kc
            slots.append(kc)
            hots.append(jnp.concatenate(
                [jnp.where(pc - CAP * m == lane, 1.0, 0.0).astype(BF16) for m in range(PPAD // CAP)], axis=1
            ))
        g = jnp.dot(jnp.concatenate(hots, axis=0), jmat[side, o], preferred_element_type=F32)
        mine = slot_of(own[side, 1, pl.ds(o, 1), :])
        ws = []
        for j in range(GROUP):
            same = slots[j] == mine
            part = g[CAP * j:CAP * (j + 1)]
            ws.append(jnp.concatenate(
                [jnp.where(same, part[:, 0:CAP], 0.0).astype(BF16), jnp.where(same, part[:, CAP:], 0.0).astype(BF16)],
                axis=1,
            ))
        u = lax.dot_general(
            jnp.concatenate(ws, axis=0), amat[side, o], (((1,), (1,)), ((), ())), preferred_element_type=F32
        )
        for j in range(GROUP):
            b = GROUP * p + j
            uh, ul = split(u[CAP * j:CAP * (j + 1)])
            hot = one_hot_rows(oth[b, 0, pl.ds(o, 1), :], BLK, oth[b, 2, pl.ds(o, 1), :].astype(F32))
            tacc[b] += jnp.dot(
                jnp.concatenate([hot, hot], axis=1), jnp.concatenate([uh, ul], axis=0), preferred_element_type=F32
            )
        at_step(it, slots_t)
        return carry

    lax.fori_loop(0, N_T, t_step, 0)

    for copy in [e for e in queue if e.q == 0]:
        take(copy)
    queue[:] = [e for e in queue if e.q == 1]

    acc[...] = jnp.zeros_like(acc)
    n_f = len(steps) // 2
    slots_f = {n: pop_until(steps[2 * n + 1][0] if n < n_f - 1 else 1e9) for n in range(n_f)}

    def f_step(it, carry):
        at_step(it, slots_f)
        lefts, rights = [], []
        for d in range(2):
            index, which = 0, 0
            for n in range(n_f):
                _, buf, rel = steps[2 * n + d]
                index = jnp.where(it == n, place(buf, 1, rel), index)
                which = jnp.where(it == n, 1 if buf == "x" else 0, which)
            left_high, left_low = split(gz[1 - which, index])
            right_high, right_low = split(gx[which, index])
            lefts += [left_high, left_high, left_low]
            rights += [right_high, right_low, right_high]
        acc[...] += jnp.dot(
            jnp.concatenate(lefts, axis=1), jnp.concatenate(rights, axis=0), preferred_element_type=F32
        )
        return carry

    lax.fori_loop(0, n_f, f_step, 0)

    sigma = acc[...]
    sigma_ref[...] = sigma
    shift = shift_ref[0]
    loads[9].wait()
    corr_ref[...] = (sigma - shift * gx[0, r]) / (diag[...] - shift)

    for copy in copies:
        describe(copy, copy.rel).wait_send()

    @pl.when(in_b)
    def _():
        for n in range(NZ - 1):
            b_copy(n, z - bz).wait_send()

    @pl.when(in_a)
    def _():
        for n in range(len(plane)):
            a_copy(n, y).wait_send()

    for jz in range(NZ // 2):
        f_copy(jz, k, False).wait_send()


def shards(coefficients, diagonal, energy_shift, integrals, source_row, target_row, phase_row,
           source_col, target_col, phase_col):
    plan = make_plan()
    n_copies = len(plan[0])
    vmem = pl.BlockSpec(memory_space=pltpu.VMEM)
    out = jax.ShapeDtypeStruct((BLK, BLK), F32)
    blocks = GROUP * PHASES
    return pl.pallas_call(
        functools.partial(kernel, plan),
        out_shape=(out, out),
        in_specs=[pl.BlockSpec(memory_space=pltpu.SMEM)] + [pl.BlockSpec(memory_space=pl.ANY)] * 9,
        out_specs=(vmem, vmem),
        scratch_shapes=[
            pltpu.VMEM((2, 16, BLK, BLK), F32),
            pltpu.VMEM((2, 16, BLK, BLK), F32),
            pltpu.VMEM((PAIRS, PAIRS), F32),
            pltpu.VMEM((BLK, BLK), F32),
            pltpu.VMEM((PPAD, PPAD), F32),
            pltpu.VMEM((2 * PPAD, PPAD), BF16),
            pltpu.VMEM((2, 3, LISTS, CAP), I32),
            pltpu.VMEM((blocks, 3, LISTS, CAP), I32),
            pltpu.VMEM((2, LISTS, PPAD, 2 * CAP), BF16),
            pltpu.VMEM((2, LISTS, BLK, 2 * CAP), BF16),
            pltpu.VMEM((blocks, LISTS, CAP, CAP), I32),
            pltpu.VMEM((blocks, BLK, BLK), F32),
            pltpu.VMEM((BLK, BLK), F32),
            pltpu.SemaphoreType.DMA((10,)),
            pltpu.SemaphoreType.DMA((n_copies,)),
            pltpu.SemaphoreType.DMA((n_copies,)),
            pltpu.SemaphoreType.DMA((15,)),
            pltpu.SemaphoreType.DMA((GROUP,)),
            pltpu.SemaphoreType.DMA((NZ - 1,)),
            pltpu.SemaphoreType.DMA((2 * GROUP,)),
            pltpu.SemaphoreType.DMA((NZ // 2,)),
        ],
        compiler_params=pltpu.CompilerParams(
            collective_id=0, has_side_effects=True, vmem_limit_bytes=60 * 1024 * 1024
        ),
    )(energy_shift, coefficients, diagonal, integrals, source_row, target_row, phase_row,
      source_col, target_col, phase_col)


def solution(mesh):
    in_specs = (
        P("row", "col"),
        P("row", "col"),
        P(),
        P(),
        P("row", None),
        P("row", None),
        P("row", None),
        P("col", None),
        P("col", None),
        P("col", None),
    )
    out_specs = (P("row", "col"), P("row", "col"))
    return jax.shard_map(shards, mesh=mesh, in_specs=in_specs, out_specs=out_specs, check_vma=False)
```

```python
import functools

import jax
import jax.numpy as jnp
from jax import lax
from jax.experimental import pallas as pl
from jax.experimental.pallas import tpu as pltpu
from jax.sharding import PartitionSpec as P

MESH = pl.DeviceIdType.MESH
NX, NY, NZ = 4, 4, 8
PAIRS = 484
PPAD = 512
BLK = 256
CAP = 128
LISTS = 16
F32, BF16, I32 = jnp.float32, jnp.bfloat16, jnp.int32


class Copy:
    def __init__(self, buf, q, rel, rows, way, deps):
        self.buf, self.q, self.rel, self.rows, self.way, self.deps = buf, q, rel, rows, way, deps
        self.number = None

    def arriving(self):
        rel = list(self.rel)
        if self.way == "s":
            rel[1] = 1 - rel[1]
        elif self.q == 1:
            rel[0] = 1 - rel[0]
        else:
            step = 1 if self.way[1] == "+" else -1
            rel[0 if self.way[0] in "xz" else 1] -= step
        return tuple(rel)


WHOLE = (0, BLK)


def plane_copies():
    copies = []

    def add(*args):
        copies.append(Copy("x", 0, *args))
        return copies[-1]

    for half, (f, g) in enumerate((("x", "y"), ("y", "x"))):
        base = half * 128
        rows, low, high = (base, 128), (base, 64), (base + 64, 64)

        def at(df, dg, f=f):
            return (df, dg) if f == "x" else (dg, df)

        own_f = [add(at(0, 0), rows, f + s, ["C"]) for s in "+-"]
        minus, plus = own_f
        spread = [(0, ["C"])]
        fwd = [add(at(-1, 0), low, f + "+", [minus]), add(at(1, 0), high, f + "-", [plus])]
        spread += [(-1, [minus]), (1, [plus]), (2, fwd)]
        for d, deps in spread:
            up = add(at(d, 0), rows, g + "+", deps)
            down = add(at(d, 0), rows, g + "-", deps)
            add(at(d, -1), low, g + "+", [up])
            add(at(d, 1), high, g + "-", [down])
    return copies


def ring_copies():
    copies = []

    def add(*args):
        copies.append(Copy("z", 0, *args))
        return copies[-1]

    have = {}
    add((0, 0), WHOLE, "s", ["C"])
    last = {}
    for half in range(2):
        rows = (half * 128, 128)
        for s, sign in (("+", -1), ("-", 1)):
            dep = ["C"]
            for t in range(3):
                copy = add((sign * t, 0), rows, "z" + s, dep)
                dep = [copy]
                have.setdefault(sign * (t + 1), []).append(copy)
            last[(half, s)] = dep
    have[4] = [add((-3, 0), (0, 128), "z+", last[(0, "+")]), add((3, 0), (128, 128), "z-", last[(1, "-")])]
    for d in (-1, 1, -2, 2, -3, 3, 4):
        add((d, 0), WHOLE, "s", have[d])
    return copies, {"z+": last[(0, "+")] + last[(1, "+")], "z-": last[(0, "-")] + last[(1, "-")]}


def block_copies(last):
    copies = []
    for j in range(GROUP):
        way = "z+" if j % 2 == 0 else "z-"
        far = Copy("z", 1, (0, 0, j), WHOLE, way, ["T0"] + last[way])
        copies += [far, Copy("z", 1, (0, 0, j), WHOLE, "s", ["T0"]), Copy("z", 1, (1, 0, j), WHOLE, "s", [far])]
    for j in range(2 * GROUP):
        way = ("x+", "x-", "y+", "y-")[j % 4]
        copies.append(Copy("x", 1, (0, j), WHOLE, way, ["T%d" % (1 + j // GROUP)]))
    return copies


RATE = {"x": 46.8, "y": 46.8, "z": 46.8, "s": 350.0}
HOP = 1.8


def simulate(copies, own_time):
    free, arrivals, pending = {}, {}, list(copies)
    while pending:
        best = None
        for copy in pending:
            times = [own_time[dep] if isinstance(dep, str) else arrivals.get(dep.number) for dep in copy.deps]
            if None in times:
                continue
            if best is None or (max(times), copy.number) < best[:2]:
                best = (max(times), copy.number, copy)
        t, _, copy = best
        start = max(t, free.get(copy.way, 0.0))
        lasting = copy.rows[1] * BLK * 4 / RATE[copy.way[0]] / 1e3
        free[copy.way] = start + lasting
        arrivals[copy.number] = start + lasting + HOP
        pending.remove(copy)
    return arrivals


GROUP = 4
PHASES = 3
N_J, J_US = 8, 0.8
ITEMS = 16 * PHASES
N_T, T_US = ITEMS // 2 + 1, 0.9
LIST_US = 5.0
T0_US = N_J * J_US + 1.5


def make_plan():
    ring, last = ring_copies()
    copies = plane_copies() + ring + block_copies(last)
    for n, copy in enumerate(copies):
        copy.number = n
    own_time = {"C": 0.0}
    for p in range(PHASES):
        own_time["T%d" % p] = T0_US + (8 * p + 9) * T_US
    arrivals = simulate(copies, own_time)
    events = sorted(copies, key=lambda c: (arrivals[c.number], c.number))
    ready = {}
    for copy in copies:
        if copy.q == 1:
            ready[(copy.buf, copy.arriving())] = arrivals[copy.number]
    steps = []
    for j in range(GROUP):
        steps.append((own_time["T0"], "z", (0, 0, j)))
    for j in range(2 * GROUP):
        steps.append((own_time["T%d" % (1 + j // GROUP)], "x", (0, j)))
    steps += [(when, buf, rel) for (buf, rel), when in ready.items()]
    steps.sort(key=lambda s: (s[0], s[1], s[2]))
    return copies, arrivals, events, steps


def split(v):
    high = v.astype(BF16)
    return high, (v - high.astype(F32)).astype(BF16)


def one_hot_rows(index_row, rows, weight=None):
    hit = lax.broadcasted_iota(I32, (rows, index_row.shape[1]), 0) == index_row
    value = 1.0 if weight is None else weight
    return jnp.where(hit, value, 0.0).astype(BF16)


def slot_of(target):
    return (target * 4333) >> 21


def kernel(
    plan,
    shift_ref, c_ref, diag_ref, int_ref,
    src_r, tgt_r, ph_r, src_c, tgt_c, ph_c,
    sigma_ref, corr_ref,
    gx, gz, ints, diag, ipad, ihl, own, oth, jmat, amat, turned, hot_0, hot_1, slot_0, slot_1, w_0, w_1, u_0, u_1,
    tacc, acc,
    load_sem, send_sem, recv_sem, a_send, a_recv, b_send, b_recv, f_send,
):
    copies, arrivals, events, steps = plan
    r, c = lax.axis_index("row"), lax.axis_index("col")
    x, y = r // NY, lax.rem(r, NY)
    z, k = c // 2, lax.rem(c, 2)
    zpar, xpar = lax.rem(z, 2), lax.rem(x + y, 2)

    def flip(v, by):
        return 1 - v if by else v

    def row_at(dx, dy):
        return lax.rem(x + (dx + NX) % NX, NX) * NY + lax.rem(y + (dy + NY) % NY, NY)

    def col_at(dz, by):
        return lax.rem(z + (dz + NZ) % NZ, NZ) * 2 + flip(k, by)

    def place(buf, q, rel):
        if q == 0:
            return row_at(*rel) if buf == "x" else col_at(*rel)
        if buf == "x":
            return 2 * GROUP * flip(xpar, rel[0]) + rel[1]
        return 2 * GROUP * flip(zpar, rel[0]) + GROUP * flip(k, rel[1]) + rel[2]

    def device(way):
        if way == "s":
            return (r, col_at(0, 1))
        d = 1 if way[1] == "+" else -1
        if way[0] == "x":
            return (row_at(d, 0), c)
        if way[0] == "y":
            return (row_at(0, d), c)
        return (r, col_at(d, 0))

    bufs = {"x": gx, "z": gz}

    def describe(copy, rel):
        where = bufs[copy.buf].at[copy.q, place(copy.buf, copy.q, rel), pl.ds(*copy.rows)]
        return pltpu.make_async_remote_copy(
            src_ref=where, dst_ref=where,
            send_sem=send_sem.at[copy.number], recv_sem=recv_sem.at[copy.number],
            device_id=device(copy.way), device_id_type=MESH,
        )

    arrived, started = set(), set()

    def start_ready():
        for copy in copies:
            if copy.number in started:
                continue
            if all((dep if isinstance(dep, str) else dep.number) in arrived for dep in copy.deps):
                started.add(copy.number)
                describe(copy, copy.rel).start()

    def have(name):
        arrived.add(name)
        start_ready()

    def take(copy):
        describe(copy, copy.arriving()).wait_recv()
        have(copy.number)

    queue = list(events)

    def pop_until(t):
        out = []
        while queue and arrivals[queue[0].number] <= t:
            out.append(queue.pop(0))
        return out

    def at_step(it, slots):
        for n, evs in slots.items():
            if evs:
                @pl.when(it == n)
                def _(evs=evs):
                    for copy in evs:
                        if callable(copy):
                            copy()
                        else:
                            take(copy)

    lists = (src_r, tgt_r, ph_r, src_c, tgt_c, ph_c)
    loads = [pltpu.make_async_copy(lists[n], own.at[n // 3, n % 3], load_sem.at[n]) for n in range(6)]
    loads.append(pltpu.make_async_copy(c_ref, gx.at[0, r], load_sem.at[6]))
    loads.append(pltpu.make_async_copy(c_ref, gz.at[0, c], load_sem.at[7]))
    loads.append(pltpu.make_async_copy(int_ref, ints, load_sem.at[8]))
    loads.append(pltpu.make_async_copy(diag_ref, diag, load_sem.at[9]))
    for load in loads:
        load.start()

    plane = [(dx, dy) for dx in range(NX) for dy in range(NY) if (dx, dy) != (0, 0)]
    peers = [(row_at(*rel), c) for rel in plane] + [(r, col_at(d, 0)) for d in range(1, NZ)] + [(r, col_at(0, 1))]
    barrier = pltpu.get_barrier_semaphore()
    for peer in peers:
        pl.semaphore_signal(barrier, inc=1, device_id=peer, device_id_type=MESH)
    for load in loads[:8]:
        load.wait()
    pl.semaphore_wait(barrier, len(peers))

    ax = 2 * zpar + k
    bz = (NZ // 2) * xpar
    in_a = x == ax
    in_b = z // (NZ // 2) == xpar

    def a_copy(n, slot):
        return pltpu.make_async_remote_copy(
            src_ref=own.at[0], dst_ref=oth.at[slot], send_sem=a_send.at[n], recv_sem=a_recv.at[slot],
            device_id=(row_at(*plane[n]), c), device_id_type=MESH,
        )

    def b_copy(n, jz):
        return pltpu.make_async_remote_copy(
            src_ref=own.at[1], dst_ref=oth.at[GROUP + 2 * jz + k], send_sem=b_send.at[n],
            recv_sem=b_recv.at[2 * jz + k],
            device_id=(r, col_at(n + 1, 0)), device_id_type=MESH,
        )

    def f_copy(jz, core, mine):
        slot = 2 * jz + core
        return pltpu.make_async_remote_copy(
            src_ref=own.at[1] if mine else oth.at[GROUP + slot], dst_ref=oth.at[GROUP + slot],
            send_sem=f_send.at[jz], recv_sem=b_recv.at[slot],
            device_id=(r, col_at(0, 1)), device_id_type=MESH,
        )

    @pl.when(in_b)
    def _():
        for n in range(NZ - 1):
            b_copy(n, z - bz).start()

    @pl.when(in_a)
    def _():
        for n in range(len(plane)):
            a_copy(n, y).start()

    def forward_lists():
        for jz in range(NZ // 2):
            @pl.when(z == bz + jz)
            def _(jz=jz):
                f_copy(jz, k, True).start()

            @pl.when(z != bz + jz)
            def _(jz=jz):
                b_copy(0, jz).wait_recv()
                f_copy(jz, k, False).start()

    ipad[...] = jnp.zeros_like(ipad)
    loads[8].wait()
    ipad[0:PAIRS, 0:PAIRS] = ints[...]
    high, low = split(ipad[...].T)
    ihl[0:PPAD, :] = high
    ihl[PPAD:, :] = low
    have("C")
    for ref in (tacc, w_0, w_1, u_0, u_1):
        ref[...] = jnp.zeros_like(ref)

    slots_j = {n: pop_until((n + 1) * J_US) for n in range(N_J)}
    slots_j[min(N_J - 1, int(LIST_US / J_US))].append(forward_lists)

    def j_step(it, carry):
        side, o0 = it // (N_J // 2), 4 * lax.rem(it, N_J // 2)
        rows = []
        for d in range(4):
            t = own[side, 1, pl.ds(o0 + d, 1), :]
            rows.append(t - PAIRS * slot_of(t))
            hot = one_hot_rows(own[side, 0, pl.ds(o0 + d, 1), :], BLK, own[side, 2, pl.ds(o0 + d, 1), :].astype(F32))
            amat[side, o0 + d, :, 0:CAP] = hot
            amat[side, o0 + d, :, CAP:] = hot
        hot = one_hot_rows(jnp.concatenate(rows, axis=1), PPAD)
        for part in range(2):
            prod = jnp.dot(ihl[pl.ds(part * PPAD, PPAD), :], hot, preferred_element_type=F32).astype(BF16)
            for d in range(4):
                jmat[side, o0 + d, :, part * CAP:(part + 1) * CAP] = prod[:, d * CAP:(d + 1) * CAP]
        at_step(it, slots_j)
        return carry

    lax.fori_loop(0, N_J, j_step, 0)

    def turn(blocks):
        for b in blocks:
            t = jnp.concatenate([oth[b, 1].astype(F32), jnp.zeros((CAP - LISTS, CAP), F32)], axis=0)
            turned[b] = t.T.astype(I32)

    for j in range(GROUP):
        @pl.when(jnp.logical_not(in_a & (y == j)))
        def _(j=j):
            a_copy(0, j).wait_recv()

    @pl.when(in_a)
    def _():
        oth[y] = own[0]

    turn(range(GROUP))

    def beta_lists():
        for jz in range(NZ // 2):
            f_copy(jz, 1 - k, False).wait_recv()

        @pl.when(in_b)
        def _():
            oth[GROUP + 2 * (z - bz) + k] = own[1]

        turn(range(GROUP, GROUP * PHASES))

    slots_t = {n: pop_until(T0_US + (n + 1) * T_US) for n in range(N_T)}
    slots_t[5].insert(0, beta_lists)

    def finish(p):
        def act():
            for j in range(GROUP):
                if p == 0:
                    gz[1, place("z", 1, (0, 0, j))] = tacc[j].T
                else:
                    gx[1, place("x", 1, (0, GROUP * (p - 1) + j))] = tacc[GROUP * p + j]
            have("T%d" % p)
        return act

    for p in range(PHASES):
        slots_t[8 * p + 8].insert(0, finish(p))

    def item_of(item):
        item = jnp.clip(item, 0, ITEMS - 1)
        p = item // 16
        return p, lax.rem(item, 16), jnp.minimum(p, 1)

    def stage_hot(item, hot_ref, slot_ref):
        p, o, _ = item_of(item)
        lane = lax.broadcasted_iota(I32, (CAP, CAP), 1)
        for j in range(GROUP):
            t = jnp.take_along_axis(turned[GROUP * p + j], jnp.full((CAP, CAP), o, I32), axis=1,
                                    mode="promise_in_bounds")
            kc = slot_of(t)
            pc = t - PAIRS * kc
            slot_ref[CAP * j:CAP * (j + 1), :] = kc
            for m in range(PPAD // CAP):
                hot = jnp.where(pc == lane + CAP * m, 1.0, 0.0).astype(BF16)
                hot_ref[CAP * j:CAP * (j + 1), CAP * m:CAP * (m + 1)] = hot

    def stage_g(item, hot_ref, slot_ref, w_ref):
        _, o, side = item_of(item)
        g = jnp.dot(hot_ref[...], jmat[side, o], preferred_element_type=F32)
        same = slot_ref[...] == slot_of(own[side, 1, pl.ds(o, 1), :])
        w_ref[:, 0:CAP] = jnp.where(same, g[:, 0:CAP], 0.0).astype(BF16)
        w_ref[:, CAP:] = jnp.where(same, g[:, CAP:], 0.0).astype(BF16)

    def stage_u(item, w_ref, u_ref):
        _, o, side = item_of(item)
        u = lax.dot_general(w_ref[...], amat[side, o], (((1,), (1,)), ((), ())), preferred_element_type=F32)
        for j in range(GROUP):
            high, low = split(u[CAP * j:CAP * (j + 1)])
            u_ref[j, 0:CAP, :] = high
            u_ref[j, CAP:, :] = low

    def stage_t(item, u_ref):
        p, o, _ = item_of(item)
        for j in range(GROUP):
            b = GROUP * p + j
            hot = one_hot_rows(oth[b, 0, pl.ds(o, 1), :], BLK, oth[b, 2, pl.ds(o, 1), :].astype(F32))
            tacc[b] += jnp.dot(jnp.concatenate([hot, hot], axis=1), u_ref[j], preferred_element_type=F32)

    stage_hot(jnp.int32(0), hot_0, slot_0)

    def t_step(n, carry):
        hots, slot_refs, ws, us = (hot_0, hot_1), (slot_0, slot_1), (w_0, w_1), (u_0, u_1)
        for d in range(2):
            it, e = 2 * n + d, 1 - d
            stage_t(it - 2, us[d])
            stage_u(it - 1, ws[e], us[e])
            stage_g(it, hots[d], slot_refs[d], ws[d])
            stage_hot(it + 1, hots[e], slot_refs[e])
        at_step(n, slots_t)
        return carry

    lax.fori_loop(0, N_T, t_step, 0)

    for copy in [e for e in queue if e.q == 0]:
        take(copy)
    queue[:] = [e for e in queue if e.q == 1]

    acc[...] = jnp.zeros_like(acc)
    n_f = len(steps) // 2
    slots_f = {n: pop_until(steps[2 * n + 1][0] if n < n_f - 1 else 1e9) for n in range(n_f)}

    def f_step(it, carry):
        at_step(it, slots_f)
        lefts, rights = [], []
        for d in range(2):
            index, which = 0, 0
            for n in range(n_f):
                _, buf, rel = steps[2 * n + d]
                index = jnp.where(it == n, place(buf, 1, rel), index)
                which = jnp.where(it == n, 1 if buf == "x" else 0, which)
            left_high, left_low = split(gz[1 - which, index])
            right_high, right_low = split(gx[which, index])
            lefts += [left_high, left_high, left_low]
            rights += [right_high, right_low, right_high]
        acc[...] += jnp.dot(
            jnp.concatenate(lefts, axis=1), jnp.concatenate(rights, axis=0), preferred_element_type=F32
        )
        return carry

    lax.fori_loop(0, n_f, f_step, 0)

    sigma = acc[...]
    sigma_ref[...] = sigma
    shift = shift_ref[0]
    loads[9].wait()
    corr_ref[...] = (sigma - shift * gx[0, r]) / (diag[...] - shift)

    for copy in copies:
        describe(copy, copy.rel).wait_send()

    @pl.when(in_b)
    def _():
        for n in range(NZ - 1):
            b_copy(n, z - bz).wait_send()

    @pl.when(in_a)
    def _():
        for n in range(len(plane)):
            a_copy(n, y).wait_send()

    for jz in range(NZ // 2):
        f_copy(jz, k, False).wait_send()


def shards(coefficients, diagonal, energy_shift, integrals, source_row, target_row, phase_row,
           source_col, target_col, phase_col):
    plan = make_plan()
    n_copies = len(plan[0])
    vmem = pl.BlockSpec(memory_space=pltpu.VMEM)
    out = jax.ShapeDtypeStruct((BLK, BLK), F32)
    blocks = GROUP * PHASES
    return pl.pallas_call(
        functools.partial(kernel, plan),
        out_shape=(out, out),
        in_specs=[pl.BlockSpec(memory_space=pltpu.SMEM)] + [pl.BlockSpec(memory_space=pl.ANY)] * 9,
        out_specs=(vmem, vmem),
        scratch_shapes=[
            pltpu.VMEM((2, 16, BLK, BLK), F32),
            pltpu.VMEM((2, 16, BLK, BLK), F32),
            pltpu.VMEM((PAIRS, PAIRS), F32),
            pltpu.VMEM((BLK, BLK), F32),
            pltpu.VMEM((PPAD, PPAD), F32),
            pltpu.VMEM((2 * PPAD, PPAD), BF16),
            pltpu.VMEM((2, 3, LISTS, CAP), I32),
            pltpu.VMEM((blocks, 3, LISTS, CAP), I32),
            pltpu.VMEM((2, LISTS, PPAD, 2 * CAP), BF16),
            pltpu.VMEM((2, LISTS, BLK, 2 * CAP), BF16),
            pltpu.VMEM((blocks, CAP, CAP), I32),
            pltpu.VMEM((GROUP * CAP, PPAD), BF16),
            pltpu.VMEM((GROUP * CAP, PPAD), BF16),
            pltpu.VMEM((GROUP * CAP, CAP), I32),
            pltpu.VMEM((GROUP * CAP, CAP), I32),
            pltpu.VMEM((GROUP * CAP, 2 * CAP), BF16),
            pltpu.VMEM((GROUP * CAP, 2 * CAP), BF16),
            pltpu.VMEM((GROUP, 2 * CAP, BLK), BF16),
            pltpu.VMEM((GROUP, 2 * CAP, BLK), BF16),
            pltpu.VMEM((blocks, BLK, BLK), F32),
            pltpu.VMEM((BLK, BLK), F32),
            pltpu.SemaphoreType.DMA((10,)),
            pltpu.SemaphoreType.DMA((n_copies,)),
            pltpu.SemaphoreType.DMA((n_copies,)),
            pltpu.SemaphoreType.DMA((15,)),
            pltpu.SemaphoreType.DMA((GROUP,)),
            pltpu.SemaphoreType.DMA((NZ - 1,)),
            pltpu.SemaphoreType.DMA((2 * GROUP,)),
            pltpu.SemaphoreType.DMA((NZ // 2,)),
        ],
        compiler_params=pltpu.CompilerParams(
            collective_id=0, has_side_effects=True, vmem_limit_bytes=60 * 1024 * 1024
        ),
    )(energy_shift, coefficients, diagonal, integrals, source_row, target_row, phase_row,
      source_col, target_col, phase_col)


def solution(mesh):
    in_specs = (
        P("row", "col"),
        P("row", "col"),
        P(),
        P(),
        P("row", None),
        P("row", None),
        P("row", None),
        P("col", None),
        P("col", None),
        P("col", None),
    )
    out_specs = (P("row", "col"), P("row", "col"))
    return jax.shard_map(shards, mesh=mesh, in_specs=in_specs, out_specs=out_specs, check_vma=False)
```

```python
import functools

import jax
import jax.numpy as jnp
from jax import lax
from jax.experimental import pallas as pl
from jax.experimental.pallas import tpu as pltpu
from jax.sharding import PartitionSpec as P

MESH = pl.DeviceIdType.MESH
NX, NY, NZ = 4, 4, 8
PAIRS = 484
PPAD = 512
BLK = 256
CAP = 128
LISTS = 16
F32, BF16, I32 = jnp.float32, jnp.bfloat16, jnp.int32


class Copy:
    def __init__(self, buf, q, rel, rows, way, deps):
        self.buf, self.q, self.rel, self.rows, self.way, self.deps = buf, q, rel, rows, way, deps
        self.number = None

    def arriving(self):
        rel = list(self.rel)
        if self.way == "s":
            rel[1] = 1 - rel[1]
        elif self.q == 1:
            rel[0] = 1 - rel[0]
        else:
            step = 1 if self.way[1] == "+" else -1
            rel[0 if self.way[0] in "xz" else 1] -= step
        return tuple(rel)


WHOLE = (0, BLK)


def plane_copies():
    copies = []

    def add(*args):
        copies.append(Copy("x", 0, *args))
        return copies[-1]

    for half, (f, g) in enumerate((("x", "y"), ("y", "x"))):
        base = half * 128
        rows, low, high = (base, 128), (base, 64), (base + 64, 64)

        def at(df, dg, f=f):
            return (df, dg) if f == "x" else (dg, df)

        own_f = [add(at(0, 0), rows, f + s, ["C"]) for s in "+-"]
        minus, plus = own_f
        spread = [(0, ["C"])]
        fwd = [add(at(-1, 0), low, f + "+", [minus]), add(at(1, 0), high, f + "-", [plus])]
        spread += [(-1, [minus]), (1, [plus]), (2, fwd)]
        for d, deps in spread:
            up = add(at(d, 0), rows, g + "+", deps)
            down = add(at(d, 0), rows, g + "-", deps)
            add(at(d, -1), low, g + "+", [up])
            add(at(d, 1), high, g + "-", [down])
    return copies


def ring_copies():
    copies = []

    def add(*args):
        copies.append(Copy("z", 0, *args))
        return copies[-1]

    have = {}
    add((0, 0), WHOLE, "s", ["C"])
    last = {}
    for half in range(2):
        rows = (half * 128, 128)
        for s, sign in (("+", -1), ("-", 1)):
            dep = ["C"]
            for t in range(3):
                copy = add((sign * t, 0), rows, "z" + s, dep)
                dep = [copy]
                have.setdefault(sign * (t + 1), []).append(copy)
            last[(half, s)] = dep
    have[4] = [add((-3, 0), (0, 128), "z+", last[(0, "+")]), add((3, 0), (128, 128), "z-", last[(1, "-")])]
    for d in (-1, 1, -2, 2, -3, 3, 4):
        add((d, 0), WHOLE, "s", have[d])
    return copies, {"z+": last[(0, "+")] + last[(1, "+")], "z-": last[(0, "-")] + last[(1, "-")]}


def block_copies(last):
    copies = []
    for j in range(GROUP):
        way = "z+" if j % 2 == 0 else "z-"
        far = Copy("z", 1, (0, 0, j), WHOLE, way, ["T0"] + last[way])
        copies += [far, Copy("z", 1, (0, 0, j), WHOLE, "s", ["T0"]), Copy("z", 1, (1, 0, j), WHOLE, "s", [far])]
    for j in range(2 * GROUP):
        way = ("x+", "x-", "y+", "y-")[j % 4]
        copies.append(Copy("x", 1, (0, j), WHOLE, way, ["T%d" % (1 + j // GROUP)]))
    return copies


RATE = {"x": 44.0, "y": 44.0, "z": 44.0, "s": 300.0}
HOP = 2.2


def simulate(copies, own_time, handled):
    free, arrivals, pending = {}, {}, list(copies)
    while pending:
        best = None
        for copy in pending:
            times = [own_time[dep] if isinstance(dep, str) else arrivals.get(dep.number) for dep in copy.deps]
            if None in times:
                continue
            if best is None or (max(times), copy.number) < best[:2]:
                best = (max(times), copy.number, copy)
        t, _, copy = best
        start = max(t, free.get(copy.way, 0.0))
        lasting = copy.rows[1] * BLK * 4 / RATE[copy.way[0]] / 1e3
        free[copy.way] = start + lasting
        arrivals[copy.number] = handled(start + lasting + HOP)
        pending.remove(copy)
    return arrivals


GROUP = 4
PHASES = 3
N_J, J_US = 8, 0.8
ITEMS = 16 * PHASES
N_T, T_US = ITEMS // 2 + 1, 1.16
LIST_US = 5.0
T0_US = N_J * J_US + 1.5
C_US = 0.0
SLOTS = [(n + 1) * J_US for n in range(N_J)] + [T0_US + (n + 1) * T_US for n in range(N_T)]


def handled(when):
    return next((slot for slot in SLOTS if slot >= when), when)


def make_plan():
    ring, last = ring_copies()
    copies = plane_copies() + ring + block_copies(last)
    for n, copy in enumerate(copies):
        copy.number = n
    own_time = {"C": C_US}
    for p in range(PHASES):
        own_time["T%d" % p] = T0_US + (8 * p + 9) * T_US
    arrivals = simulate(copies, own_time, handled)
    events = sorted(copies, key=lambda c: (arrivals[c.number], c.number))
    ready = {}
    for copy in copies:
        if copy.q == 1:
            ready[(copy.buf, copy.arriving())] = arrivals[copy.number]
    steps = []
    for j in range(GROUP):
        steps.append((own_time["T0"], "z", (0, 0, j)))
    for j in range(2 * GROUP):
        steps.append((own_time["T%d" % (1 + j // GROUP)], "x", (0, j)))
    steps += [(when, buf, rel) for (buf, rel), when in ready.items()]
    steps.sort(key=lambda s: (s[0], s[1], s[2]))
    return copies, arrivals, events, steps


def split(v):
    high = v.astype(BF16)
    return high, (v - high.astype(F32)).astype(BF16)


def one_hot_rows(index_row, rows, weight=None):
    hit = lax.broadcasted_iota(I32, (rows, index_row.shape[1]), 0) == index_row
    value = 1.0 if weight is None else weight
    return jnp.where(hit, value, 0.0).astype(BF16)


def slot_of(target):
    return (target * 4333) >> 21


def kernel(
    plan,
    shift_ref, c_ref, diag_ref, int_ref,
    src_r, tgt_r, ph_r, src_c, tgt_c, ph_c,
    sigma_ref, corr_ref,
    gx, gz, ints, diag, ipad, ihl, own, oth, jmat, amat, turned, hot_0, hot_1, slot_0, slot_1, w_0, w_1, u_0, u_1,
    tacc, acc,
    load_sem, send_sem, recv_sem, a_send, a_recv, b_send, b_recv, f_send,
):
    copies, arrivals, events, steps = plan
    r, c = lax.axis_index("row"), lax.axis_index("col")
    x, y = r // NY, lax.rem(r, NY)
    z, k = c // 2, lax.rem(c, 2)
    zpar, xpar = lax.rem(z, 2), lax.rem(x + y, 2)

    def flip(v, by):
        return 1 - v if by else v

    xs = [lax.rem(x + d, NX) * NY for d in range(NX)]
    ys = [lax.rem(y + d, NY) for d in range(NY)]
    zs = [lax.rem(z + d, NZ) * 2 for d in range(NZ)]
    ks = [k, 1 - k]
    rows_at = {(i, j): xs[i] + ys[j] for i in range(NX) for j in range(NY)}
    cols_at = {(i, j): zs[i] + ks[j] for i in range(NZ) for j in range(2)}
    x_base = [2 * GROUP * flip(xpar, i) for i in range(2)]
    z_base = {(i, j): 2 * GROUP * flip(zpar, i) + GROUP * ks[j] for i in range(2) for j in range(2)}

    def row_at(dx, dy):
        return rows_at[(dx % NX, dy % NY)]

    def col_at(dz, by):
        return cols_at[(dz % NZ, by)]

    def place(buf, q, rel):
        if q == 0:
            return row_at(*rel) if buf == "x" else col_at(*rel)
        return x_base[rel[0]] + rel[1] if buf == "x" else z_base[rel[:2]] + rel[2]

    def device(way):
        if way == "s":
            return (r, col_at(0, 1))
        d = 1 if way[1] == "+" else -1
        if way[0] == "x":
            return (row_at(d, 0), c)
        if way[0] == "y":
            return (row_at(0, d), c)
        return (r, col_at(d, 0))

    bufs = {"x": gx, "z": gz}

    def describe(copy, rel):
        where = bufs[copy.buf].at[copy.q, place(copy.buf, copy.q, rel), pl.ds(*copy.rows)]
        return pltpu.make_async_remote_copy(
            src_ref=where, dst_ref=where,
            send_sem=send_sem.at[copy.number], recv_sem=recv_sem.at[copy.number],
            device_id=device(copy.way), device_id_type=MESH,
        )

    arrived, started = set(), set()

    def start_ready():
        for copy in copies:
            if copy.number in started:
                continue
            if all((dep if isinstance(dep, str) else dep.number) in arrived for dep in copy.deps):
                started.add(copy.number)
                describe(copy, copy.rel).start()

    def have(name):
        arrived.add(name)
        start_ready()

    def take(copy):
        describe(copy, copy.arriving()).wait_recv()
        have(copy.number)

    queue = list(events)

    def pop_until(t):
        out = []
        while queue and arrivals[queue[0].number] <= t:
            out.append(queue.pop(0))
        return out

    def at_step(it, slots):
        def act(evs):
            for event in evs:
                if callable(event):
                    event()
                else:
                    take(event)

        def walk(low, high):
            filled = [n for n in range(low, high) if slots[n]]
            if not filled:
                return
            if high - low == 1:
                act(slots[low])
                return
            if len(filled) == 1:
                pl.when(it == filled[0])(lambda: act(slots[filled[0]]))
                return
            mid = filled[len(filled) // 2]

            def lower():
                walk(low, mid)

            def upper():
                walk(mid, high)

            lax.cond(it < mid, lower, upper)

        walk(0, len(slots))

    lists = (src_r, tgt_r, ph_r, src_c, tgt_c, ph_c)
    loads = [pltpu.make_async_copy(lists[n], own.at[n // 3, n % 3], load_sem.at[n]) for n in range(6)]
    loads.append(pltpu.make_async_copy(c_ref, gx.at[0, r], load_sem.at[6]))
    loads.append(pltpu.make_async_copy(c_ref, gz.at[0, c], load_sem.at[7]))
    loads.append(pltpu.make_async_copy(int_ref, ints, load_sem.at[8]))
    loads.append(pltpu.make_async_copy(diag_ref, diag, load_sem.at[9]))
    for load in loads:
        load.start()

    plane = [(dx, dy) for dx in range(NX) for dy in range(NY) if (dx, dy) != (0, 0)]
    peers = [(row_at(*rel), c) for rel in plane] + [(r, col_at(d, 0)) for d in range(1, NZ)] + [(r, col_at(0, 1))]
    barrier = pltpu.get_barrier_semaphore()
    for peer in peers:
        pl.semaphore_signal(barrier, inc=1, device_id=peer, device_id_type=MESH)
    for load in loads[:8]:
        load.wait()
    pl.semaphore_wait(barrier, len(peers))

    ax = 2 * zpar + k
    bz = (NZ // 2) * xpar
    in_a = x == ax
    in_b = z // (NZ // 2) == xpar

    def a_copy(n, slot):
        return pltpu.make_async_remote_copy(
            src_ref=own.at[0], dst_ref=oth.at[slot], send_sem=a_send.at[n], recv_sem=a_recv.at[slot],
            device_id=(row_at(*plane[n]), c), device_id_type=MESH,
        )

    def b_copy(n, jz):
        return pltpu.make_async_remote_copy(
            src_ref=own.at[1], dst_ref=oth.at[GROUP + 2 * jz + k], send_sem=b_send.at[n],
            recv_sem=b_recv.at[2 * jz + k],
            device_id=(r, col_at(n + 1, 0)), device_id_type=MESH,
        )

    def f_copy(jz, core, mine):
        slot = 2 * jz + core
        return pltpu.make_async_remote_copy(
            src_ref=own.at[1] if mine else oth.at[GROUP + slot], dst_ref=oth.at[GROUP + slot],
            send_sem=f_send.at[jz], recv_sem=b_recv.at[slot],
            device_id=(r, col_at(0, 1)), device_id_type=MESH,
        )

    @pl.when(in_b)
    def _():
        for n in range(NZ - 1):
            b_copy(n, z - bz).start()

    @pl.when(in_a)
    def _():
        for n in range(len(plane)):
            a_copy(n, y).start()

    def forward_lists():
        for jz in range(NZ // 2):
            @pl.when(z == bz + jz)
            def _(jz=jz):
                f_copy(jz, k, True).start()

            @pl.when(z != bz + jz)
            def _(jz=jz):
                b_copy(0, jz).wait_recv()
                f_copy(jz, k, False).start()

    ipad[...] = jnp.zeros_like(ipad)
    loads[8].wait()
    ipad[0:PAIRS, 0:PAIRS] = ints[...]
    high, low = split(ipad[...].T)
    ihl[0:PPAD, :] = high
    ihl[PPAD:, :] = low
    have("C")
    for ref in (tacc, w_0, w_1, u_0, u_1):
        ref[...] = jnp.zeros_like(ref)

    slots_j = {n: pop_until((n + 1) * J_US) for n in range(N_J)}
    slots_j[min(N_J - 1, int(LIST_US / J_US))].append(forward_lists)

    def j_step(it, carry):
        side, o0 = it // (N_J // 2), 4 * lax.rem(it, N_J // 2)
        rows = []
        for d in range(4):
            t = own[side, 1, pl.ds(o0 + d, 1), :]
            rows.append(t - PAIRS * slot_of(t))
            hot = one_hot_rows(own[side, 0, pl.ds(o0 + d, 1), :], BLK, own[side, 2, pl.ds(o0 + d, 1), :].astype(F32))
            amat[side, o0 + d, :, 0:CAP] = hot
            amat[side, o0 + d, :, CAP:] = hot
        hot = one_hot_rows(jnp.concatenate(rows, axis=1), PPAD)
        for part in range(2):
            prod = jnp.dot(ihl[pl.ds(part * PPAD, PPAD), :], hot, preferred_element_type=F32).astype(BF16)
            for d in range(4):
                jmat[side, o0 + d, :, part * CAP:(part + 1) * CAP] = prod[:, d * CAP:(d + 1) * CAP]
        at_step(it, slots_j)
        return carry

    lax.fori_loop(0, N_J, j_step, 0)

    def turn(blocks):
        for b in blocks:
            t = jnp.concatenate([oth[b, 1].astype(F32), jnp.zeros((CAP - LISTS, CAP), F32)], axis=0)
            turned[b] = t.T.astype(I32)

    for j in range(GROUP):
        @pl.when(jnp.logical_not(in_a & (y == j)))
        def _(j=j):
            a_copy(0, j).wait_recv()

    @pl.when(in_a)
    def _():
        oth[y] = own[0]

    turn(range(GROUP))

    def beta_lists():
        for jz in range(NZ // 2):
            f_copy(jz, 1 - k, False).wait_recv()

        @pl.when(in_b)
        def _():
            oth[GROUP + 2 * (z - bz) + k] = own[1]

        turn(range(GROUP, GROUP * PHASES))

    slots_t = {n: pop_until(T0_US + (n + 1) * T_US) for n in range(N_T)}
    slots_t[5].insert(0, beta_lists)

    def finish(p):
        def act():
            for j in range(GROUP):
                if p == 0:
                    gz[1, place("z", 1, (0, 0, j))] = tacc[j].T
                else:
                    gx[1, place("x", 1, (0, GROUP * (p - 1) + j))] = tacc[GROUP * p + j]
            have("T%d" % p)
        return act

    for p in range(PHASES):
        slots_t[8 * p + 8].insert(0, finish(p))

    def item_of(item):
        item = jnp.clip(item, 0, ITEMS - 1)
        p = item // 16
        return p, lax.rem(item, 16), jnp.minimum(p, 1)

    def stage_hot(item, hot_ref, slot_ref):
        p, o, _ = item_of(item)
        lane = lax.broadcasted_iota(I32, (CAP, CAP), 1)
        for j in range(GROUP):
            t = jnp.take_along_axis(turned[GROUP * p + j], jnp.full((CAP, CAP), o, I32), axis=1,
                                    mode="promise_in_bounds")
            kc = slot_of(t)
            pc = t - PAIRS * kc
            slot_ref[CAP * j:CAP * (j + 1), :] = kc
            for m in range(PPAD // CAP):
                hot = jnp.where(pc == lane + CAP * m, 1.0, 0.0).astype(BF16)
                hot_ref[CAP * j:CAP * (j + 1), CAP * m:CAP * (m + 1)] = hot

    def stage_g(item, hot_ref, slot_ref, w_ref):
        _, o, side = item_of(item)
        g = jnp.dot(hot_ref[...], jmat[side, o], preferred_element_type=F32)
        same = slot_ref[...] == slot_of(own[side, 1, pl.ds(o, 1), :])
        w_ref[:, 0:CAP] = jnp.where(same, g[:, 0:CAP], 0.0).astype(BF16)
        w_ref[:, CAP:] = jnp.where(same, g[:, CAP:], 0.0).astype(BF16)

    def stage_u(item, w_ref, u_ref):
        _, o, side = item_of(item)
        u = lax.dot_general(w_ref[...], amat[side, o], (((1,), (1,)), ((), ())), preferred_element_type=F32)
        for j in range(GROUP):
            high, low = split(u[CAP * j:CAP * (j + 1)])
            u_ref[j, 0:CAP, :] = high
            u_ref[j, CAP:, :] = low

    def stage_t(item, u_ref):
        p, o, _ = item_of(item)
        for j in range(GROUP):
            b = GROUP * p + j
            hot = one_hot_rows(oth[b, 0, pl.ds(o, 1), :], BLK, oth[b, 2, pl.ds(o, 1), :].astype(F32))
            tacc[b] += jnp.dot(jnp.concatenate([hot, hot], axis=1), u_ref[j], preferred_element_type=F32)

    stage_hot(jnp.int32(0), hot_0, slot_0)

    def t_step(n, carry):
        hots, slot_refs, ws, us = (hot_0, hot_1), (slot_0, slot_1), (w_0, w_1), (u_0, u_1)
        for d in range(2):
            it, e = 2 * n + d, 1 - d
            stage_t(it - 2, us[d])
            stage_u(it - 1, ws[e], us[e])
            stage_g(it, hots[d], slot_refs[d], ws[d])
            stage_hot(it + 1, hots[e], slot_refs[e])
        at_step(n, slots_t)
        return carry

    lax.fori_loop(0, N_T, t_step, 0)

    for copy in [e for e in queue if e.q == 0]:
        take(copy)
    queue[:] = [e for e in queue if e.q == 1]

    acc[...] = jnp.zeros_like(acc)
    n_f = len(steps) // 2
    slots_f = {n: pop_until(steps[2 * n + 1][0] if n < n_f - 1 else 1e9) for n in range(n_f)}

    def f_step(it, carry):
        at_step(it, slots_f)
        lefts, rights = [], []
        for d in range(2):
            index, which = 0, 0
            for n in range(n_f):
                _, buf, rel = steps[2 * n + d]
                index = jnp.where(it == n, place(buf, 1, rel), index)
                which = jnp.where(it == n, 1 if buf == "x" else 0, which)
            left_high, left_low = split(gz[1 - which, index])
            right_high, right_low = split(gx[which, index])
            lefts += [left_high, left_high, left_low]
            rights += [right_high, right_low, right_high]
        acc[...] += jnp.dot(
            jnp.concatenate(lefts, axis=1), jnp.concatenate(rights, axis=0), preferred_element_type=F32
        )
        return carry

    lax.fori_loop(0, n_f, f_step, 0)

    sigma = acc[...]
    sigma_ref[...] = sigma
    shift = shift_ref[0]
    loads[9].wait()
    corr_ref[...] = (sigma - shift * gx[0, r]) / (diag[...] - shift)

    for copy in copies:
        describe(copy, copy.rel).wait_send()

    @pl.when(in_b)
    def _():
        for n in range(NZ - 1):
            b_copy(n, z - bz).wait_send()

    @pl.when(in_a)
    def _():
        for n in range(len(plane)):
            a_copy(n, y).wait_send()

    for jz in range(NZ // 2):
        f_copy(jz, k, False).wait_send()


def shards(coefficients, diagonal, energy_shift, integrals, source_row, target_row, phase_row,
           source_col, target_col, phase_col):
    plan = make_plan()
    n_copies = len(plan[0])
    vmem = pl.BlockSpec(memory_space=pltpu.VMEM)
    out = jax.ShapeDtypeStruct((BLK, BLK), F32)
    blocks = GROUP * PHASES
    return pl.pallas_call(
        functools.partial(kernel, plan),
        out_shape=(out, out),
        in_specs=[pl.BlockSpec(memory_space=pltpu.SMEM)] + [pl.BlockSpec(memory_space=pl.ANY)] * 9,
        out_specs=(vmem, vmem),
        scratch_shapes=[
            pltpu.VMEM((2, 16, BLK, BLK), F32),
            pltpu.VMEM((2, 16, BLK, BLK), F32),
            pltpu.VMEM((PAIRS, PAIRS), F32),
            pltpu.VMEM((BLK, BLK), F32),
            pltpu.VMEM((PPAD, PPAD), F32),
            pltpu.VMEM((2 * PPAD, PPAD), BF16),
            pltpu.VMEM((2, 3, LISTS, CAP), I32),
            pltpu.VMEM((blocks, 3, LISTS, CAP), I32),
            pltpu.VMEM((2, LISTS, PPAD, 2 * CAP), BF16),
            pltpu.VMEM((2, LISTS, BLK, 2 * CAP), BF16),
            pltpu.VMEM((blocks, CAP, CAP), I32),
            pltpu.VMEM((GROUP * CAP, PPAD), BF16),
            pltpu.VMEM((GROUP * CAP, PPAD), BF16),
            pltpu.VMEM((GROUP * CAP, CAP), I32),
            pltpu.VMEM((GROUP * CAP, CAP), I32),
            pltpu.VMEM((GROUP * CAP, 2 * CAP), BF16),
            pltpu.VMEM((GROUP * CAP, 2 * CAP), BF16),
            pltpu.VMEM((GROUP, 2 * CAP, BLK), BF16),
            pltpu.VMEM((GROUP, 2 * CAP, BLK), BF16),
            pltpu.VMEM((blocks, BLK, BLK), F32),
            pltpu.VMEM((BLK, BLK), F32),
            pltpu.SemaphoreType.DMA((10,)),
            pltpu.SemaphoreType.DMA((n_copies,)),
            pltpu.SemaphoreType.DMA((n_copies,)),
            pltpu.SemaphoreType.DMA((15,)),
            pltpu.SemaphoreType.DMA((GROUP,)),
            pltpu.SemaphoreType.DMA((NZ - 1,)),
            pltpu.SemaphoreType.DMA((2 * GROUP,)),
            pltpu.SemaphoreType.DMA((NZ // 2,)),
        ],
        compiler_params=pltpu.CompilerParams(
            collective_id=0, has_side_effects=True, vmem_limit_bytes=60 * 1024 * 1024
        ),
    )(energy_shift, coefficients, diagonal, integrals, source_row, target_row, phase_row,
      source_col, target_col, phase_col)


def solution(mesh):
    in_specs = (
        P("row", "col"),
        P("row", "col"),
        P(),
        P(),
        P("row", None),
        P("row", None),
        P("row", None),
        P("col", None),
        P("col", None),
        P("col", None),
    )
    out_specs = (P("row", "col"), P("row", "col"))
    return jax.shard_map(shards, mesh=mesh, in_specs=in_specs, out_specs=out_specs, check_vma=False)
```

```python
import functools

import jax
import jax.numpy as jnp
from jax import lax
from jax.experimental import pallas as pl
from jax.experimental.pallas import tpu as pltpu
from jax.sharding import PartitionSpec as P

MESH = pl.DeviceIdType.MESH
NX, NY, NZ = 4, 4, 8
PAIRS = 484
PPAD = 512
BLK = 256
CAP = 128
LISTS = 16
F32, BF16, I32 = jnp.float32, jnp.bfloat16, jnp.int32


class Copy:
    def __init__(self, buf, q, rel, rows, way, deps):
        self.buf, self.q, self.rel, self.rows, self.way, self.deps = buf, q, rel, rows, way, deps
        self.number = None

    def arriving(self):
        rel = list(self.rel)
        if self.way == "s":
            rel[1] = 1 - rel[1]
        elif self.q == 1:
            rel[0] = 1 - rel[0]
        else:
            step = 1 if self.way[1] == "+" else -1
            rel[0 if self.way[0] in "xz" else 1] -= step
        return tuple(rel)


WHOLE = (0, BLK)


def plane_copies():
    copies = []

    def add(*args):
        copies.append(Copy("x", 0, *args))
        return copies[-1]

    for half, (f, g) in enumerate((("x", "y"), ("y", "x"))):
        base = half * 128
        rows, low, high = (base, 128), (base, 64), (base + 64, 64)

        def at(df, dg, f=f):
            return (df, dg) if f == "x" else (dg, df)

        own_f = [add(at(0, 0), rows, f + s, ["C"]) for s in "+-"]
        minus, plus = own_f
        spread = [(0, ["C"])]
        fwd = [add(at(-1, 0), low, f + "+", [minus]), add(at(1, 0), high, f + "-", [plus])]
        spread += [(-1, [minus]), (1, [plus]), (2, fwd)]
        for d, deps in spread:
            up = add(at(d, 0), rows, g + "+", deps)
            down = add(at(d, 0), rows, g + "-", deps)
            add(at(d, -1), low, g + "+", [up])
            add(at(d, 1), high, g + "-", [down])
    return copies


def ring_copies():
    copies = []

    def add(*args):
        copies.append(Copy("z", 0, *args))
        return copies[-1]

    have = {}
    add((0, 0), WHOLE, "s", ["C"])
    last = {}
    for half in range(2):
        rows = (half * 128, 128)
        for s, sign in (("+", -1), ("-", 1)):
            dep = ["C"]
            for t in range(3):
                copy = add((sign * t, 0), rows, "z" + s, dep)
                dep = [copy]
                have.setdefault(sign * (t + 1), []).append(copy)
            last[(half, s)] = dep
    have[4] = [add((-3, 0), (0, 128), "z+", last[(0, "+")]), add((3, 0), (128, 128), "z-", last[(1, "-")])]
    for d in (-1, 1, -2, 2, -3, 3, 4):
        add((d, 0), WHOLE, "s", have[d])
    return copies, {"z+": last[(0, "+")] + last[(1, "+")], "z-": last[(0, "-")] + last[(1, "-")]}


def block_copies(last):
    copies = []
    for j in range(GROUP):
        way = "z+" if j % 2 == 0 else "z-"
        far = Copy("z", 1, (0, 0, j), WHOLE, way, ["T0"] + last[way])
        copies += [far, Copy("z", 1, (0, 0, j), WHOLE, "s", ["T0"]), Copy("z", 1, (1, 0, j), WHOLE, "s", [far])]
    for j in range(2 * GROUP):
        way = ("x+", "x-", "y+", "y-")[j % 4]
        copies.append(Copy("x", 1, (0, j), WHOLE, way, ["T%d" % (1 + j // GROUP)]))
    return copies


RATE = {"x": 38.0, "y": 38.0, "z": 38.0, "s": 300.0}
HOP = 3.5


def simulate(copies, own_time, handled):
    free, arrivals, pending = {}, {}, list(copies)
    while pending:
        best = None
        for copy in pending:
            times = [own_time[dep] if isinstance(dep, str) else arrivals.get(dep.number) for dep in copy.deps]
            if None in times:
                continue
            if best is None or (max(times), copy.number) < best[:2]:
                best = (max(times), copy.number, copy)
        t, _, copy = best
        start = max(t, free.get(copy.way, 0.0))
        lasting = copy.rows[1] * BLK * 4 / RATE[copy.way[0]] / 1e3
        free[copy.way] = start + lasting
        arrivals[copy.number] = handled(start + lasting + HOP)
        pending.remove(copy)
    return arrivals


GROUP = 4
PHASES = 3
N_J, J_US = 8, 0.8
ITEMS = 16 * PHASES
N_T, T_US = ITEMS // 2 + 1, 1.16
LIST_US = 5.0
T0_US = N_J * J_US + 1.5
C_US = 0.0
SLOTS = [(n + 1) * J_US for n in range(N_J)] + [T0_US + (n + 1) * T_US for n in range(N_T)]


def handled(when):
    return next((slot for slot in SLOTS if slot >= when), when)


def make_plan():
    ring, last = ring_copies()
    copies = plane_copies() + ring + block_copies(last)
    for n, copy in enumerate(copies):
        copy.number = n
    own_time = {"C": C_US}
    for p in range(PHASES):
        own_time["T%d" % p] = T0_US + (8 * p + 9) * T_US
    arrivals = simulate(copies, own_time, handled)
    events = sorted(copies, key=lambda c: (arrivals[c.number], c.number))
    ready = {}
    for copy in copies:
        if copy.q == 1:
            ready[(copy.buf, copy.arriving())] = arrivals[copy.number]
    steps = []
    for j in range(GROUP):
        steps.append((own_time["T0"], "z", (0, 0, j)))
    for j in range(2 * GROUP):
        steps.append((own_time["T%d" % (1 + j // GROUP)], "x", (0, j)))
    steps += [(when, buf, rel) for (buf, rel), when in ready.items()]
    steps.sort(key=lambda s: (s[0], s[1], s[2]))
    return copies, arrivals, events, steps


def split(v):
    high = v.astype(BF16)
    return high, (v - high.astype(F32)).astype(BF16)


def one_hot_rows(index_row, rows, weight=None):
    hit = lax.broadcasted_iota(I32, (rows, index_row.shape[1]), 0) == index_row
    value = 1.0 if weight is None else weight
    return jnp.where(hit, value, 0.0).astype(BF16)


def slot_of(target):
    return (target * 4333) >> 21


def kernel(
    plan,
    shift_ref, c_ref, diag_ref, int_ref,
    src_r, tgt_r, ph_r, src_c, tgt_c, ph_c,
    sigma_ref, corr_ref,
    gx, gz, ints, diag, ipad, ihl, own, oth, jmat, amat, turned, hot_0, hot_1, slot_0, slot_1, w_0, w_1, u_0, u_1,
    tacc, acc,
    load_sem, send_sem, recv_sem, a_send, a_recv, b_send, b_recv, f_send,
):
    copies, arrivals, events, steps = plan
    r, c = lax.axis_index("row"), lax.axis_index("col")
    x, y = r // NY, lax.rem(r, NY)
    z, k = c // 2, lax.rem(c, 2)
    zpar, xpar = lax.rem(z, 2), lax.rem(x + y, 2)

    def flip(v, by):
        return 1 - v if by else v

    xs = [lax.rem(x + d, NX) * NY for d in range(NX)]
    ys = [lax.rem(y + d, NY) for d in range(NY)]
    zs = [lax.rem(z + d, NZ) * 2 for d in range(NZ)]
    ks = [k, 1 - k]
    rows_at = {(i, j): xs[i] + ys[j] for i in range(NX) for j in range(NY)}
    cols_at = {(i, j): zs[i] + ks[j] for i in range(NZ) for j in range(2)}
    x_base = [2 * GROUP * flip(xpar, i) for i in range(2)]
    z_base = {(i, j): 2 * GROUP * flip(zpar, i) + GROUP * ks[j] for i in range(2) for j in range(2)}

    def row_at(dx, dy):
        return rows_at[(dx % NX, dy % NY)]

    def col_at(dz, by):
        return cols_at[(dz % NZ, by)]

    def place(buf, q, rel):
        if q == 0:
            return row_at(*rel) if buf == "x" else col_at(*rel)
        return x_base[rel[0]] + rel[1] if buf == "x" else z_base[rel[:2]] + rel[2]

    def device(way):
        if way == "s":
            return (r, col_at(0, 1))
        d = 1 if way[1] == "+" else -1
        if way[0] == "x":
            return (row_at(d, 0), c)
        if way[0] == "y":
            return (row_at(0, d), c)
        return (r, col_at(d, 0))

    bufs = {"x": gx, "z": gz}

    def describe(copy, rel):
        where = bufs[copy.buf].at[copy.q, place(copy.buf, copy.q, rel), pl.ds(*copy.rows)]
        return pltpu.make_async_remote_copy(
            src_ref=where, dst_ref=where,
            send_sem=send_sem.at[copy.number], recv_sem=recv_sem.at[copy.number],
            device_id=device(copy.way), device_id_type=MESH,
        )

    arrived, started = set(), set()

    def start_ready():
        for copy in copies:
            if copy.number in started:
                continue
            if all((dep if isinstance(dep, str) else dep.number) in arrived for dep in copy.deps):
                started.add(copy.number)
                describe(copy, copy.rel).start()

    def have(name):
        arrived.add(name)
        start_ready()

    def take(copy):
        describe(copy, copy.arriving()).wait_recv()
        have(copy.number)

    queue = list(events)

    def pop_until(t):
        out = []
        while queue and arrivals[queue[0].number] <= t:
            out.append(queue.pop(0))
        return out

    def at_step(it, slots):
        def act(evs):
            for event in evs:
                if callable(event):
                    event()
                else:
                    take(event)

        def walk(low, high):
            filled = [n for n in range(low, high) if slots[n]]
            if not filled:
                return
            if high - low == 1:
                act(slots[low])
                return
            if len(filled) == 1:
                pl.when(it == filled[0])(lambda: act(slots[filled[0]]))
                return
            mid = filled[len(filled) // 2]

            def lower():
                walk(low, mid)

            def upper():
                walk(mid, high)

            lax.cond(it < mid, lower, upper)

        walk(0, len(slots))

    lists = (src_r, tgt_r, ph_r, src_c, tgt_c, ph_c)
    loads = [pltpu.make_async_copy(lists[n], own.at[n // 3, n % 3], load_sem.at[n]) for n in range(6)]
    loads.append(pltpu.make_async_copy(c_ref, gx.at[0, r], load_sem.at[6]))
    loads.append(pltpu.make_async_copy(c_ref, gz.at[0, c], load_sem.at[7]))
    loads.append(pltpu.make_async_copy(int_ref, ints, load_sem.at[8]))
    loads.append(pltpu.make_async_copy(diag_ref, diag, load_sem.at[9]))
    for load in loads:
        load.start()

    plane = [(dx, dy) for dx in range(NX) for dy in range(NY) if (dx, dy) != (0, 0)]
    peers = [(row_at(*rel), c) for rel in plane] + [(r, col_at(d, 0)) for d in range(1, NZ)] + [(r, col_at(0, 1))]
    barrier = pltpu.get_barrier_semaphore()
    for peer in peers:
        pl.semaphore_signal(barrier, inc=1, device_id=peer, device_id_type=MESH)
    for load in loads[:8]:
        load.wait()
    pl.semaphore_wait(barrier, len(peers))

    ax = 2 * zpar + k
    bz = (NZ // 2) * xpar
    in_a = x == ax
    in_b = z // (NZ // 2) == xpar

    def a_copy(n, slot):
        return pltpu.make_async_remote_copy(
            src_ref=own.at[0], dst_ref=oth.at[slot], send_sem=a_send.at[n], recv_sem=a_recv.at[slot],
            device_id=(row_at(*plane[n]), c), device_id_type=MESH,
        )

    def b_copy(n, jz):
        return pltpu.make_async_remote_copy(
            src_ref=own.at[1], dst_ref=oth.at[GROUP + 2 * jz + k], send_sem=b_send.at[n],
            recv_sem=b_recv.at[2 * jz + k],
            device_id=(r, col_at(n + 1, 0)), device_id_type=MESH,
        )

    def f_copy(jz, core, mine):
        slot = 2 * jz + core
        return pltpu.make_async_remote_copy(
            src_ref=own.at[1] if mine else oth.at[GROUP + slot], dst_ref=oth.at[GROUP + slot],
            send_sem=f_send.at[jz], recv_sem=b_recv.at[slot],
            device_id=(r, col_at(0, 1)), device_id_type=MESH,
        )

    @pl.when(in_b)
    def _():
        for n in range(NZ - 1):
            b_copy(n, z - bz).start()

    @pl.when(in_a)
    def _():
        for n in range(len(plane)):
            a_copy(n, y).start()

    def forward_lists():
        for jz in range(NZ // 2):
            @pl.when(z == bz + jz)
            def _(jz=jz):
                f_copy(jz, k, True).start()

            @pl.when(z != bz + jz)
            def _(jz=jz):
                b_copy(0, jz).wait_recv()
                f_copy(jz, k, False).start()

    ipad[...] = jnp.zeros_like(ipad)
    loads[8].wait()
    ipad[0:PAIRS, 0:PAIRS] = ints[...]
    high, low = split(ipad[...].T)
    ihl[0:PPAD, :] = high
    ihl[PPAD:, :] = low
    have("C")
    for ref in (tacc, w_0, w_1, u_0, u_1):
        ref[...] = jnp.zeros_like(ref)

    slots_j = {n: pop_until((n + 1) * J_US) for n in range(N_J)}
    slots_j[min(N_J - 1, int(LIST_US / J_US))].append(forward_lists)

    def j_step(it, carry):
        side, o0 = it // (N_J // 2), 4 * lax.rem(it, N_J // 2)
        rows = []
        for d in range(4):
            t = own[side, 1, pl.ds(o0 + d, 1), :]
            rows.append(t - PAIRS * slot_of(t))
            hot = one_hot_rows(own[side, 0, pl.ds(o0 + d, 1), :], BLK, own[side, 2, pl.ds(o0 + d, 1), :].astype(F32))
            amat[side, o0 + d, :, 0:CAP] = hot
            amat[side, o0 + d, :, CAP:] = hot
        hot = one_hot_rows(jnp.concatenate(rows, axis=1), PPAD)
        for part in range(2):
            prod = jnp.dot(ihl[pl.ds(part * PPAD, PPAD), :], hot, preferred_element_type=F32).astype(BF16)
            for d in range(4):
                jmat[side, o0 + d, :, part * CAP:(part + 1) * CAP] = prod[:, d * CAP:(d + 1) * CAP]
        at_step(it, slots_j)
        return carry

    lax.fori_loop(0, N_J, j_step, 0)

    def turn(blocks):
        for b in blocks:
            t = jnp.concatenate([oth[b, 1].astype(F32), jnp.zeros((CAP - LISTS, CAP), F32)], axis=0)
            turned[b] = t.T.astype(I32)

    for j in range(GROUP):
        @pl.when(jnp.logical_not(in_a & (y == j)))
        def _(j=j):
            a_copy(0, j).wait_recv()

    @pl.when(in_a)
    def _():
        oth[y] = own[0]

    turn(range(GROUP))

    def beta_lists():
        for jz in range(NZ // 2):
            f_copy(jz, 1 - k, False).wait_recv()

        @pl.when(in_b)
        def _():
            oth[GROUP + 2 * (z - bz) + k] = own[1]

        turn(range(GROUP, GROUP * PHASES))

    slots_t = {n: pop_until(T0_US + (n + 1) * T_US) for n in range(N_T)}
    slots_t[5].insert(0, beta_lists)

    def finish(p):
        def act():
            for j in range(GROUP):
                if p == 0:
                    gz[1, place("z", 1, (0, 0, j))] = tacc[j].T
                else:
                    gx[1, place("x", 1, (0, GROUP * (p - 1) + j))] = tacc[GROUP * p + j]
            have("T%d" % p)
        return act

    for p in range(PHASES):
        slots_t[8 * p + 8].insert(0, finish(p))

    def item_of(item):
        item = jnp.clip(item, 0, ITEMS - 1)
        p = item // 16
        return p, lax.rem(item, 16), jnp.minimum(p, 1)

    def stage_hot(item, hot_ref, slot_ref):
        p, o, _ = item_of(item)
        lane = lax.broadcasted_iota(I32, (CAP, CAP), 1)
        for j in range(GROUP):
            t = jnp.take_along_axis(turned[GROUP * p + j], jnp.full((CAP, CAP), o, I32), axis=1,
                                    mode="promise_in_bounds")
            kc = slot_of(t)
            pc = t - PAIRS * kc
            slot_ref[CAP * j:CAP * (j + 1), :] = kc
            for m in range(PPAD // CAP):
                hot = jnp.where(pc == lane + CAP * m, 1.0, 0.0).astype(BF16)
                hot_ref[CAP * j:CAP * (j + 1), CAP * m:CAP * (m + 1)] = hot

    def stage_g(item, hot_ref, slot_ref, w_ref):
        _, o, side = item_of(item)
        g = jnp.dot(hot_ref[...], jmat[side, o], preferred_element_type=F32)
        same = slot_ref[...] == slot_of(own[side, 1, pl.ds(o, 1), :])
        w_ref[:, 0:CAP] = jnp.where(same, g[:, 0:CAP], 0.0).astype(BF16)
        w_ref[:, CAP:] = jnp.where(same, g[:, CAP:], 0.0).astype(BF16)

    def stage_u(item, w_ref, u_ref):
        _, o, side = item_of(item)
        u = lax.dot_general(w_ref[...], amat[side, o], (((1,), (1,)), ((), ())), preferred_element_type=F32)
        for j in range(GROUP):
            high, low = split(u[CAP * j:CAP * (j + 1)])
            u_ref[j, 0:CAP, :] = high
            u_ref[j, CAP:, :] = low

    def stage_t(item, u_ref):
        p, o, _ = item_of(item)
        for j in range(GROUP):
            b = GROUP * p + j
            hot = one_hot_rows(oth[b, 0, pl.ds(o, 1), :], BLK, oth[b, 2, pl.ds(o, 1), :].astype(F32))
            tacc[b] += jnp.dot(jnp.concatenate([hot, hot], axis=1), u_ref[j], preferred_element_type=F32)

    stage_hot(jnp.int32(0), hot_0, slot_0)

    def t_step(n, carry):
        hots, slot_refs, ws, us = (hot_0, hot_1), (slot_0, slot_1), (w_0, w_1), (u_0, u_1)
        for d in range(2):
            it, e = 2 * n + d, 1 - d
            stage_t(it - 2, us[d])
            stage_u(it - 1, ws[e], us[e])
            stage_g(it, hots[d], slot_refs[d], ws[d])
            stage_hot(it + 1, hots[e], slot_refs[e])
        at_step(n, slots_t)
        return carry

    lax.fori_loop(0, N_T, t_step, 0)

    for copy in [e for e in queue if e.q == 0]:
        take(copy)
    queue[:] = [e for e in queue if e.q == 1]

    acc[...] = jnp.zeros_like(acc)
    n_f = len(steps) // 2
    slots_f = {n: pop_until(steps[2 * n + 1][0] if n < n_f - 1 else 1e9) for n in range(n_f)}

    def f_step(it, carry):
        at_step(it, slots_f)
        lefts, rights = [], []
        for d in range(2):
            index, which = 0, 0
            for n in range(n_f):
                _, buf, rel = steps[2 * n + d]
                index = jnp.where(it == n, place(buf, 1, rel), index)
                which = jnp.where(it == n, 1 if buf == "x" else 0, which)
            left_high, left_low = split(gz[1 - which, index])
            right_high, right_low = split(gx[which, index])
            lefts += [left_high, left_high, left_low]
            rights += [right_high, right_low, right_high]
        acc[...] += jnp.dot(
            jnp.concatenate(lefts, axis=1), jnp.concatenate(rights, axis=0), preferred_element_type=F32
        )
        return carry

    lax.fori_loop(0, n_f, f_step, 0)

    sigma = acc[...]
    sigma_ref[...] = sigma
    shift = shift_ref[0]
    loads[9].wait()
    corr_ref[...] = (sigma - shift * gx[0, r]) / (diag[...] - shift)

    for copy in copies:
        describe(copy, copy.rel).wait_send()

    @pl.when(in_b)
    def _():
        for n in range(NZ - 1):
            b_copy(n, z - bz).wait_send()

    @pl.when(in_a)
    def _():
        for n in range(len(plane)):
            a_copy(n, y).wait_send()

    for jz in range(NZ // 2):
        f_copy(jz, k, False).wait_send()


def shards(coefficients, diagonal, energy_shift, integrals, source_row, target_row, phase_row,
           source_col, target_col, phase_col):
    plan = make_plan()
    n_copies = len(plan[0])
    vmem = pl.BlockSpec(memory_space=pltpu.VMEM)
    out = jax.ShapeDtypeStruct((BLK, BLK), F32)
    blocks = GROUP * PHASES
    return pl.pallas_call(
        functools.partial(kernel, plan),
        out_shape=(out, out),
        in_specs=[pl.BlockSpec(memory_space=pltpu.SMEM)] + [pl.BlockSpec(memory_space=pl.ANY)] * 9,
        out_specs=(vmem, vmem),
        scratch_shapes=[
            pltpu.VMEM((2, 16, BLK, BLK), F32),
            pltpu.VMEM((2, 16, BLK, BLK), F32),
            pltpu.VMEM((PAIRS, PAIRS), F32),
            pltpu.VMEM((BLK, BLK), F32),
            pltpu.VMEM((PPAD, PPAD), F32),
            pltpu.VMEM((2 * PPAD, PPAD), BF16),
            pltpu.VMEM((2, 3, LISTS, CAP), I32),
            pltpu.VMEM((blocks, 3, LISTS, CAP), I32),
            pltpu.VMEM((2, LISTS, PPAD, 2 * CAP), BF16),
            pltpu.VMEM((2, LISTS, BLK, 2 * CAP), BF16),
            pltpu.VMEM((blocks, CAP, CAP), I32),
            pltpu.VMEM((GROUP * CAP, PPAD), BF16),
            pltpu.VMEM((GROUP * CAP, PPAD), BF16),
            pltpu.VMEM((GROUP * CAP, CAP), I32),
            pltpu.VMEM((GROUP * CAP, CAP), I32),
            pltpu.VMEM((GROUP * CAP, 2 * CAP), BF16),
            pltpu.VMEM((GROUP * CAP, 2 * CAP), BF16),
            pltpu.VMEM((GROUP, 2 * CAP, BLK), BF16),
            pltpu.VMEM((GROUP, 2 * CAP, BLK), BF16),
            pltpu.VMEM((blocks, BLK, BLK), F32),
            pltpu.VMEM((BLK, BLK), F32),
            pltpu.SemaphoreType.DMA((10,)),
            pltpu.SemaphoreType.DMA((n_copies,)),
            pltpu.SemaphoreType.DMA((n_copies,)),
            pltpu.SemaphoreType.DMA((15,)),
            pltpu.SemaphoreType.DMA((GROUP,)),
            pltpu.SemaphoreType.DMA((NZ - 1,)),
            pltpu.SemaphoreType.DMA((2 * GROUP,)),
            pltpu.SemaphoreType.DMA((NZ // 2,)),
        ],
        compiler_params=pltpu.CompilerParams(
            collective_id=0, has_side_effects=True, vmem_limit_bytes=60 * 1024 * 1024
        ),
    )(energy_shift, coefficients, diagonal, integrals, source_row, target_row, phase_row,
      source_col, target_col, phase_col)


def solution(mesh):
    in_specs = (
        P("row", "col"),
        P("row", "col"),
        P(),
        P(),
        P("row", None),
        P("row", None),
        P("row", None),
        P("col", None),
        P("col", None),
        P("col", None),
    )
    out_specs = (P("row", "col"), P("row", "col"))
    return jax.shard_map(shards, mesh=mesh, in_specs=in_specs, out_specs=out_specs, check_vma=False)
```
